768 devices in a mesh: mem: 32 (over y, x_hi, core), lat: 24 (over x_lo, z).
Axes of the slice: x: 4 (x_hi: 2, x_lo: 2; x = x_hi * 2 + x_lo), y: 8, z: 12, core: 2. Of those that a mesh axis runs over, the one named last changes fastest.
Arguments:
- ensemble: float32 [256, 4, 96, 1024], P('mem', None, 'lat'), may hold values from -6 to 6
- obs_value: float32 [1, 768, 16], P(None, ('mem', 'lat')), may hold values from -9 to 9
- obs_var: float32 [1, 768, 16], P(None, ('mem', 'lat')), may hold values from 0.5 to 4
- obs_cell: int32 [1, 768, 16], P(None, ('mem', 'lat')), may hold values from 0 to 511
- obs_loop: int32 [1, 768, 16], P(None, ('mem', 'lat')), may hold values from 0 to 3
- obs_count: int32 [1, 768], P(None, ('mem', 'lat')), may hold values from 8 to 16, as said below
Outputs:
- analysis: float32 [256, 4, 96, 1024], P('mem', None, 'lat')
The draws below stay inside these ranges and needn't reach their ends.
Inputs may be any that keep to these rules, and one draw needn't show every extreme that they name: `obs_count`: at least 8 and at most 16 slots live per patch; in each cycle some patch has all 16 slots live and another exactly 8.
All inputs are finite; a program needn't handle non-finite values.
Results may differ from the reference program's by a relative error of at most 0.0003.
Values sent between devices are 32-bit elements; how exact they have to be, the bound alone decides.
A program may use at most 32 MiB of HBM per device.

```python
import math
import jax
import jax.numpy as jnp
from jax import lax

K = 256
F = 4
NX = 1024
ROWS = 4
NOBS = 16
NCYC = 1
STEPS = 1
NSI = 5
NY = 96
NPATCH = 768
CELLS = 512
N_MEM = 32
N_LAT = 24


def draw_obs_count(key, part):
    key_base, key_top, key_offset = jax.random.split(jax.random.fold_in(key, 7), 3)
    base = jax.random.randint(key_base, (NCYC, NPATCH), NOBS // 2, NOBS + 1)
    top_patch = jax.random.randint(key_top, (NCYC,), 0, NPATCH)
    offset = jax.random.randint(key_offset, (NCYC,), 1, NPATCH)
    low_patch = (top_patch + offset) % NPATCH
    patch_index = jnp.arange(NPATCH)[None, :]
    base = jnp.where(patch_index == top_patch[:, None], NOBS, base)
    base = jnp.where(patch_index == low_patch[:, None], NOBS // 2, base)
    return base.astype(jnp.int32)


def with_ends(values, stream_key, least, largest):
    shape = values.shape
    place = [jax.random.randint(jax.random.fold_in(stream_key, axis), (), 0, shape[axis]) for axis in range(len(shape))]
    values = values.at[tuple(place)].set(least)
    longest = shape.index(max(shape))
    place[longest] = (place[longest] + 1) % shape[longest]
    return values.at[tuple(place)].set(largest)


def level_of(own_key, extent, cuts, least, top_value):
    level = 1.0
    for position, blocks in cuts:
        heights = jax.random.uniform(jax.random.fold_in(jax.random.fold_in(own_key, 6), position), (blocks,), jnp.float32, least / len(cuts), top_value / len(cuts))
        level = level * jnp.repeat(jnp.exp(heights), extent[position] // blocks).reshape((-1,) + (1,) * (len(extent) - 1 - position))
    return level


def normal_values(rng, dims, deviation, most, pieces=(), held_as=jnp.bfloat16):
    values = deviation * jax.random.normal(rng, dims, jnp.float32)
    if pieces:
        values = values * level_of(rng, dims, pieces, -0.22, 0.18)
    return jnp.clip(values, -most, most).astype(held_as)


def setup_inputs(seed: int = 0) -> dict:
    splits = jax.random.split(jax.random.key(seed), 7)
    return {
        "ensemble": normal_values(splits[0], (K, F, NY, NX), 1.0, 6.0, ((0, 32), (2, 24)), jnp.float32),
        "obs_value": normal_values(splits[1], (NCYC, NPATCH, NOBS), 1.5, 9.0, ((1, 768),), jnp.float32),
        "obs_var": jnp.clip(jnp.exp(math.log(4.0) - 2.0794415 * jax.random.uniform(splits[2], (NCYC, NPATCH, NOBS), jnp.float32) ** level_of(splits[2], (NCYC, NPATCH, NOBS), ((1, 768),), -0.2, 0.2)), 0.5, 4.0),
        "obs_cell": with_ends(jax.random.randint(splits[3], (NCYC, NPATCH, NOBS), 0, CELLS), jax.random.fold_in(splits[3], 1), 0, CELLS - 1).astype(jnp.int32),
        "obs_loop": with_ends(jax.random.randint(splits[4], (NCYC, NPATCH, NOBS), 0, 4), jax.random.fold_in(splits[4], 1), 0, 3).astype(jnp.int32),
        "obs_count": draw_obs_count(jax.random.fold_in(splits[6], 71), 0),
    }


time_step = 0.15
viscosity = 0.1
third_part = 1.0 / 3.0
two_thirds = 2.0 / 3.0

def tendency(padded):
    centre = padded[:, :, 1:-1, 1:-1]
    to_north = padded[:, :, 2:, 1:-1]
    to_south = padded[:, :, :-2, 1:-1]
    to_east = padded[:, :, 1:-1, 2:]
    to_west = padded[:, :, 1:-1, :-2]
    zonal_wind = centre[:, 0:1]
    meridional = centre[:, 1:2]
    moved = zonal_wind * (to_east - to_west) * 0.5 + meridional * (to_north - to_south) * 0.5
    return -moved + viscosity * (to_north + to_south + to_east + to_west - 4.0 * centre)

def extend_fixed(state):
    padded = jnp.pad(state, ((0, 0), (0, 0), (1, 1), (0, 0)))
    return jnp.concatenate([padded[..., -1:], padded, padded[..., :1]], axis=3)

def advance(state):
    first = state + time_step * tendency(extend_fixed(state))
    second = 0.75 * state + 0.25 * (first + time_step * tendency(extend_fixed(first)))
    return third_part * state + two_thirds * (second + time_step * tendency(extend_fixed(second)))

def analyse(cells, values, variance, slot_cell, slot_loop, count):
    members = cells.shape[0]
    highest = lax.Precision.HIGHEST
    centre_mean = lax.optimization_barrier(jnp.mean(cells, axis=0))
    perturb = cells - centre_mean
    seen = jnp.take(cells, slot_cell, axis=1)
    seen_mean = lax.optimization_barrier(jnp.mean(seen, axis=0))
    seen_pert = seen - seen_mean
    slots = jnp.arange(slot_cell.shape[0], dtype=jnp.int32)
    weight = jnp.where(slots < count, jnp.exp(-0.35 * slot_loop.astype(cells.dtype)) / variance, 0.0)
    scaled = seen_pert * weight
    gram = jnp.dot(scaled, seen_pert.T, precision=highest)
    drive = jnp.dot(scaled, values - seen_mean, precision=highest)
    identity = jnp.eye(members, dtype=cells.dtype)
    bound = members - 1.0 + 0.5 * jnp.trace(gram)
    root_up = ((members - 1.0) * identity + gram) / bound
    root_down = identity
    for repeat in range(NSI):
        factor = 1.5 * identity - 0.5 * jnp.dot(root_down, root_up, precision=highest)
        root_up = jnp.dot(root_up, factor, precision=highest)
        root_down = jnp.dot(factor, root_down, precision=highest)
    spread = root_down * jnp.sqrt((members - 1.0) / bound)
    centre_shift = jnp.dot(root_down, jnp.dot(root_down, drive, precision=highest), precision=highest) / bound
    transform = spread + centre_shift[:, None]
    return centre_mean + jnp.dot(transform.T, perturb, precision=highest)

def reference(ensemble, obs_value, obs_var, obs_cell, obs_loop, obs_count):
    state = ensemble
    members, fields, rows_all, columns = state.shape
    lon_part = columns // N_MEM

    def one_patch(packed):
        return analyse(*packed)
    for cycle_index in range(NCYC):
        for repeat in range(STEPS):
            state = advance(state)
        blocks = state.reshape(members, fields, N_LAT, ROWS, N_MEM, lon_part)
        blocks = blocks.transpose(4, 2, 0, 1, 3, 5).reshape(N_MEM * N_LAT, members, fields * ROWS * lon_part)
        result = lax.map(one_patch, (blocks, obs_value[cycle_index], obs_var[cycle_index], obs_cell[cycle_index], obs_loop[cycle_index], obs_count[cycle_index]))
        result = result.reshape(N_MEM, N_LAT, members, fields, ROWS, lon_part)
        state = result.transpose(2, 3, 1, 4, 0, 5).reshape(members, fields, rows_all, columns)
    return state
```

```python
import functools

import jax
import jax.numpy as jnp
from jax import lax
from jax.experimental import pallas as pl
from jax.experimental.pallas import tpu as pltpu
from jax.sharding import PartitionSpec as P

MESH = pl.DeviceIdType.MESH
NSI = 5
DT = 0.15
VISC = 0.1


def mm(a, b, dims=((1,), (0,))):
    return lax.dot_general(
        a, b, (dims, ((), ())), precision=lax.Precision.HIGHEST, preferred_element_type=jnp.float32
    )


def stage(source, base, target, rows, shift, weight_base, weight_mid):
    width = source.shape[-1]

    def row(i, _):
        u = source[i + 1, 0]
        v = source[i + 1, 1]
        scale = weight_mid * DT
        east_w = scale * VISC - (0.5 * scale) * u
        west_w = scale * VISC + (0.5 * scale) * u
        north_w = scale * VISC - (0.5 * scale) * v
        south_w = scale * VISC + (0.5 * scale) * v
        for f in range(4):
            c = source[i + 1, f]
            total = (weight_mid - 4.0 * scale * VISC) * c
            total += north_w * source[i + 2, f] + south_w * source[i, f]
            total += east_w * pltpu.roll(c, width - 1, 1) + west_w * pltpu.roll(c, 1, 1)
            if weight_base:
                total += weight_base * base[i + shift, f]
            target[i, f] = total
        return 0

    lax.fori_loop(0, rows, row, 0)


def analysis_weights(ypt, pert, onehot, xbar, values, variance, loop, count, members):
    nobs = ypt.shape[0]
    eye = (
        lax.broadcasted_iota(jnp.int32, (nobs, nobs), 0)
        == lax.broadcasted_iota(jnp.int32, (nobs, nobs), 1)
    )
    identity = jnp.where(eye, 1.0, 0.0)
    slots = lax.broadcasted_iota(jnp.int32, (1, nobs), 1)
    weight = jnp.where(slots < count, jnp.exp(-0.35 * loop) / variance, 0.0)

    def column(row):
        return jnp.sum(jnp.where(eye, row, 0.0), axis=1, keepdims=True)

    weight_col = column(weight)
    seen_mean = jnp.sum(onehot * xbar, axis=1, keepdims=True)
    innovation = column(values) - seen_mean
    cross = mm(ypt, pert)
    gram = mm(ypt, ypt, ((1,), (1,)))
    trace = jnp.sum(jnp.where(eye, gram * weight, 0.0), axis=(0, 1), keepdims=True)
    bound = members - 1.0 + 0.5 * trace
    a = (members - 1.0) / bound
    t = gram * weight / bound
    p0, p_m, p_h = a, a * identity + t, identity
    z0, z_m, z_h = jnp.ones_like(a), identity, jnp.zeros_like(identity)
    for repeat in range(NSI):
        g0 = 1.5 - 0.5 * p0
        g_m = 1.5 * identity - 0.5 * p_m
        g_h = -0.5 * p_h
        if repeat == 0:
            z_m, z_h, z0 = g_m, g_h, g0
            pg_m = mm(p_m, g_m)
            pg_h = g_m + p0 * g_h
        else:
            prod = mm(jnp.concatenate([p_m, p_h, z_m, z_h], axis=0), g_m)
            pg_m = prod[0:nobs]
            pg_h = prod[nobs : 2 * nobs] + p0 * g_h
            z_m = prod[2 * nobs : 3 * nobs]
            z_h = prod[3 * nobs :] + z0 * g_h
            z0 = z0 * g0
        if repeat < NSI - 1:
            prod = mm(jnp.concatenate([pg_m, pg_h], axis=0), g_m)
            p_m = prod[0:nobs]
            p_h = prod[nobs:] + (p0 * g0) * g_h
            p0 = p0 * g0 * g0
    spread = jnp.sqrt(a)
    step = mm(z_m, mm(z_m, innovation))
    shift_row = jnp.sum(weight_col * step * cross, axis=0, keepdims=True) / bound
    rows = mm((spread / bound) * weight_col * z_h, cross)
    return spread * z0, rows, xbar + shift_row


def kernel(
    x_ref, values_ref, variance_ref, cell_ref, loop_ref, count_ref, o_ref,
    wide, mid, mid2, last, packed, gathered, fresh, back,
    halo_send, halo_recv, send_a, recv_a, send_b, recv_b,
):
    n_mem, n_lat = lax.axis_size("mem"), lax.axis_size("lat")
    me, band = lax.axis_index("mem"), lax.axis_index("lat")
    north, south = lax.rem(band + 1, n_lat), lax.rem(band + n_lat - 1, n_lat)
    members, fields, rows, width = x_ref.shape
    group = n_mem // 8

    barrier = pltpu.get_barrier_semaphore()

    def greet(k, _):
        pl.semaphore_signal(
            barrier, inc=1, device_id={"mem": lax.rem(me + k, n_mem)}, device_id_type=MESH
        )
        return 0

    pl.semaphore_signal(barrier, inc=1, device_id={"lat": north}, device_id_type=MESH)
    pl.semaphore_signal(barrier, inc=1, device_id={"lat": south}, device_id_type=MESH)
    lax.fori_loop(1, n_mem, greet, 0)

    for r in range(rows):
        for f in range(fields):
            wide[3 + r, f] = x_ref[:, f, r, :]

    pl.semaphore_wait(barrier, n_mem + 1)

    upward = pltpu.make_async_remote_copy(
        src_ref=wide.at[pl.ds(rows, 3)], dst_ref=wide.at[pl.ds(0, 3)],
        send_sem=halo_send.at[0], recv_sem=halo_recv.at[0],
        device_id={"lat": north}, device_id_type=MESH,
    )
    downward = pltpu.make_async_remote_copy(
        src_ref=wide.at[pl.ds(3, 3)], dst_ref=wide.at[pl.ds(3 + rows, 3)],
        send_sem=halo_send.at[1], recv_sem=halo_recv.at[1],
        device_id={"lat": south}, device_id_type=MESH,
    )
    upward.start()
    downward.start()
    upward.wait()
    downward.wait()

    def clear(ref, start, size):
        ref[pl.ds(start, size)] = jnp.zeros((size,) + ref.shape[1:], ref.dtype)

    def clear_outside(ref, extra):
        @pl.when(band == 0)
        def _():
            clear(ref, 0, extra)

        @pl.when(band == n_lat - 1)
        def _():
            clear(ref, extra + rows, extra)

    clear_outside(wide, 3)
    stage(wide, None, mid, rows + 4, 0, 0.0, 1.0)
    clear_outside(mid, 2)
    stage(mid, wide, mid2, rows + 2, 2, 0.75, 0.25)
    clear_outside(mid2, 1)
    stage(mid2, wide, last, rows, 3, 1.0 / 3.0, 2.0 / 3.0)

    part = width // n_mem
    per_block = 128 // part
    lane = lax.broadcasted_iota(jnp.int32, (members, 128), 1) // part

    def choose(pieces, offset):
        out = pieces[0] if offset == 0 else pltpu.roll(pieces[0], (-offset * part) % 128, 1)
        for r in range(1, rows):
            turned = pltpu.roll(pieces[r], ((r - offset) * part) % 128, 1) if r != offset else pieces[r]
            out = jnp.where(lane == r, turned, out)
        return out

    def pack(j, _):
        columns = pl.ds(pl.multiple_of(j * 128, 128), 128)
        for f in range(fields):
            pieces = [last[r, f, :, columns] for r in range(rows)]
            for q in range(per_block):
                packed[j * per_block + q, :, pl.ds(f * 128, 128)] = choose(pieces, q)
        return 0

    lax.fori_loop(0, width // 128, pack, 0)

    def exchange(source, target, send_sem, recv_sem):
        def send(i, _):
            peer = lax.rem(me + 1 + lax.rem(i + n_mem // 2 - 1, n_mem - 1), n_mem)
            pltpu.make_async_remote_copy(
                src_ref=source.at[peer], dst_ref=target.at[me],
                send_sem=send_sem, recv_sem=recv_sem,
                device_id={"mem": peer}, device_id_type=MESH,
            ).start()
            return 0

        lax.fori_loop(0, n_mem - 1, send, 0)
        target[me] = source[me]
        others = pl.ds(0, n_mem - 1)
        pltpu.make_async_copy(target.at[others], target.at[others], recv_sem).wait()

    def drain(source, send_sem):
        others = pl.ds(0, n_mem - 1)
        pltpu.make_async_copy(source.at[others], source.at[others], send_sem).wait()

    exchange(packed, gathered, send_a, recv_a)

    total = n_mem * members
    cells = fields * rows * part
    values_all = gathered[...].reshape(total, cells)
    xbar = jnp.sum(values_all, axis=0, keepdims=True) * (1.0 / total)
    pert = values_all - xbar
    nobs = values_ref.shape[1]
    eye = (
        lax.broadcasted_iota(jnp.int32, (nobs, nobs), 0)
        == lax.broadcasted_iota(jnp.int32, (nobs, nobs), 1)
    )
    cell = cell_ref[...].astype(jnp.float32)
    cell_col = jnp.sum(jnp.where(eye, cell, 0.0), axis=1, keepdims=True).astype(jnp.int32)
    onehot = jnp.where(lax.broadcasted_iota(jnp.int32, (nobs, cells), 1) == cell_col, 1.0, 0.0)
    ypt = mm(onehot, pert, ((1,), (1,)))
    yp = mm(pert, onehot, ((1,), (1,)))
    kept, on_obs, common = analysis_weights(
        ypt, pert, onehot, xbar, values_ref[...], variance_ref[...],
        loop_ref[...].astype(jnp.float32), count_ref[...], float(total),
    )
    updated = kept * pert + mm(yp, on_obs) + common
    fresh[...] = updated.reshape(n_mem, members, cells)
    exchange(fresh, back, send_b, recv_b)

    def unpack(j, _):
        columns = pl.ds(pl.multiple_of(j * 128, 128), 128)
        for f in range(fields):
            pieces = [back[j * per_block + q, :, pl.ds(f * 128, 128)] for q in range(per_block)]
            for r in range(rows):
                o_ref[:, f, r, columns] = choose(pieces, r)
        return 0

    lax.fori_loop(0, width // 128, unpack, 0)
    drain(packed, send_a)
    drain(fresh, send_b)


def per_device(ensemble, obs_value, obs_var, obs_cell, obs_loop, obs_count):
    members, fields, rows, width = ensemble.shape
    n_mem = lax.axis_size("mem")
    cells = fields * rows * width // n_mem
    f32 = jnp.float32
    vmem = pl.BlockSpec(memory_space=pltpu.VMEM)
    return pl.pallas_call(
        kernel,
        out_shape=jax.ShapeDtypeStruct(ensemble.shape, f32),
        in_specs=[vmem] * 6,
        out_specs=vmem,
        scratch_shapes=[
            pltpu.VMEM((rows + 6, fields, members, width), f32),
            pltpu.VMEM((rows + 4, fields, members, width), f32),
            pltpu.VMEM((rows + 2, fields, members, width), f32),
            pltpu.VMEM((rows, fields, members, width), f32),
            pltpu.VMEM((n_mem, members, cells), f32),
            pltpu.VMEM((n_mem, members, cells), f32),
            pltpu.VMEM((n_mem, members, cells), f32),
            pltpu.VMEM((n_mem, members, cells), f32),
            pltpu.SemaphoreType.DMA((2,)),
            pltpu.SemaphoreType.DMA((2,)),
            pltpu.SemaphoreType.DMA,
            pltpu.SemaphoreType.DMA,
            pltpu.SemaphoreType.DMA,
            pltpu.SemaphoreType.DMA,
        ],
        compiler_params=pltpu.CompilerParams(collective_id=0, has_side_effects=True),
    )(
        ensemble, obs_value[0], obs_var[0], obs_cell[0], obs_loop[0], obs_count,
    )


def solution(mesh):
    placed = (
        P("mem", None, "lat", None),
        P(None, ("mem", "lat"), None),
        P(None, ("mem", "lat"), None),
        P(None, ("mem", "lat"), None),
        P(None, ("mem", "lat"), None),
        P(None, ("mem", "lat")),
    )
    return jax.shard_map(
        per_device,
        mesh=mesh,
        in_specs=placed,
        out_specs=P("mem", None, "lat", None),
        check_vma=False,
    )
```

```python
import jax
import jax.numpy as jnp
from jax import lax
from jax.experimental import pallas as pl
from jax.experimental.pallas import tpu as pltpu
from jax.sharding import PartitionSpec as P

MESH = pl.DeviceIdType.MESH
NSI = 5
DT = 0.15
VISC = 0.1
CHUNK = 2
HALO = 3


def mm(a, b, dims=((1,), (0,))):
    return lax.dot_general(
        a, b, (dims, ((), ())), precision=lax.Precision.HIGHEST, preferred_element_type=jnp.float32
    )


def analysis_weights(ypt, pert, onehot, xbar, values, variance, loop, count, members):
    nobs = ypt.shape[0]
    eye = (
        lax.broadcasted_iota(jnp.int32, (nobs, nobs), 0)
        == lax.broadcasted_iota(jnp.int32, (nobs, nobs), 1)
    )
    identity = jnp.where(eye, 1.0, 0.0)
    slots = lax.broadcasted_iota(jnp.int32, (1, nobs), 1)
    weight = jnp.where(slots < count, jnp.exp(-0.35 * loop) / variance, 0.0)

    def column(row):
        return jnp.sum(jnp.where(eye, row, 0.0), axis=1, keepdims=True)

    weight_col = column(weight)
    seen_mean = jnp.sum(onehot * xbar, axis=1, keepdims=True)
    innovation = column(values) - seen_mean
    cross = mm(ypt, pert)
    gram = mm(ypt, ypt, ((1,), (1,)))
    trace = jnp.sum(jnp.where(eye, gram * weight, 0.0), axis=(0, 1), keepdims=True)
    bound = members - 1.0 + 0.5 * trace
    a = (members - 1.0) / bound
    t = gram * weight / bound
    p0, p_m, p_h = a, a * identity + t, identity
    z0, z_m, z_h = jnp.ones_like(a), identity, jnp.zeros_like(identity)
    for repeat in range(NSI):
        g0 = 1.5 - 0.5 * p0
        g_m = 1.5 * identity - 0.5 * p_m
        g_h = -0.5 * p_h
        if repeat == 0:
            z_m, z_h, z0 = g_m, g_h, g0
            pg_m = mm(p_m, g_m)
            pg_h = g_m + p0 * g_h
        else:
            prod = mm(jnp.concatenate([p_m, p_h, z_m, z_h], axis=0), g_m)
            pg_m = prod[0:nobs]
            pg_h = prod[nobs : 2 * nobs] + p0 * g_h
            z_m = prod[2 * nobs : 3 * nobs]
            z_h = prod[3 * nobs :] + z0 * g_h
            z0 = z0 * g0
        if repeat < NSI - 1:
            prod = mm(jnp.concatenate([pg_m, pg_h], axis=0), g_m)
            p_m = prod[0:nobs]
            p_h = prod[nobs:] + (p0 * g0) * g_h
            p0 = p0 * g0 * g0
    spread = jnp.sqrt(a)
    step = mm(z_m, mm(z_m, innovation))
    shift_row = jnp.sum(weight_col * step * cross, axis=0, keepdims=True) / bound
    rows = mm((spread / bound) * weight_col * z_h, cross)
    return spread * z0, rows, xbar + shift_row


def kernel(
    x_ref, values_ref, variance_ref, cell_ref, loop_ref, count_ref, o_ref,
    wide, mid, mid2, packed, gathered, fresh, back,
    halo_send, halo_recv, send_a, recv_a, send_b, recv_b,
):
    n_mem, n_lat = lax.axis_size("mem"), lax.axis_size("lat")
    me, band = lax.axis_index("mem"), lax.axis_index("lat")
    members, fields, _, _ = x_ref.shape
    rows = 4
    chunks = members // CHUNK
    spans = packed.shape[2]
    held = fields // spans

    barrier = pltpu.get_barrier_semaphore()

    def greet(k, _):
        pl.semaphore_signal(
            barrier, inc=1, device_id={"mem": lax.rem(me + k, n_mem)}, device_id_type=MESH
        )
        return 0

    @pl.when(band < n_lat - 1)
    def _():
        pl.semaphore_signal(barrier, inc=1, device_id={"lat": band + 1}, device_id_type=MESH)

    @pl.when(band > 0)
    def _():
        pl.semaphore_signal(barrier, inc=1, device_id={"lat": band - 1}, device_id_type=MESH)

    lax.fori_loop(1, n_mem, greet, 0)

    def spread_rows(m, _):
        for f in range(fields):
            for r in range(rows):
                wide[m, HALO + r, f] = x_ref[m, f, pl.ds(r, 8, stride=rows), :]
        return 0

    lax.fori_loop(0, members, spread_rows, 0)

    beside = (band + n_lat - 1) // n_lat + (2 * n_lat - 2 - band) // n_lat
    pl.semaphore_wait(barrier, n_mem - 1 + beside)

    def upward(c):
        part = pl.ds(c * CHUNK, CHUNK)
        return pltpu.make_async_remote_copy(
            src_ref=wide.at[part, pl.ds(rows, HALO)], dst_ref=wide.at[part, pl.ds(0, HALO)],
            send_sem=halo_send.at[0, c], recv_sem=halo_recv.at[0, c],
            device_id={"lat": band + 1}, device_id_type=MESH,
        )

    def downward(c):
        part = pl.ds(c * CHUNK, CHUNK)
        return pltpu.make_async_remote_copy(
            src_ref=wide.at[part, pl.ds(HALO, HALO)], dst_ref=wide.at[part, pl.ds(HALO + rows, HALO)],
            send_sem=halo_send.at[1, c], recv_sem=halo_recv.at[1, c],
            device_id={"lat": band - 1}, device_id_type=MESH,
        )

    @pl.when(band < n_lat - 1)
    def _():
        for c in range(chunks):
            upward(c).start()

    @pl.when(band > 0)
    def _():
        for c in range(chunks):
            downward(c).start()

    lane = lax.broadcasted_iota(jnp.int32, (8, 128), 1)
    last_lane, first_lane = lane == 127, lane == 0
    quarter = lane // 32
    has_south, has_north = band > 0, band < n_lat - 1

    def east(c):
        turned = pltpu.roll(c, 127, 1)
        return jnp.where(last_lane, pltpu.roll(turned, 7, 0), turned)

    def west(c):
        turned = pltpu.roll(c, 1, 1)
        return jnp.where(first_lane, pltpu.roll(turned, 1, 0), turned)

    def stage(source, base, count, weight_base, weight_mid):
        scale = weight_mid * DT
        for i in range(count):
            u = 0.5 * scale * source(i + 1, 0)
            v = 0.5 * scale * source(i + 1, 1)
            drag = scale * VISC
            east_w, west_w, north_w, south_w = drag - u, drag + u, drag - v, drag + v
            for f in range(fields):
                c = source(i + 1, f)
                total = (weight_mid - 4.0 * drag) * c
                total += north_w * source(i + 2, f) + south_w * source(i, f)
                total += east_w * east(c) + west_w * west(c)
                if weight_base:
                    total += weight_base * base(i, f)
                yield i, f, total

    def inside(value, i, extra):
        if i < extra:
            return jnp.where(has_south, value, 0.0)
        if i >= extra + rows:
            return jnp.where(has_north, value, 0.0)
        return value

    def choose(pieces, offset):
        out = None
        for r in range(rows):
            turned = pltpu.roll(pieces[r], ((r - offset) * 32) % 128, 1) if r != offset else pieces[r]
            out = turned if out is None else jnp.where(quarter == r, turned, out)
        return out

    def position(slot):
        return lax.rem(slot, rows), pl.ds(pl.multiple_of((slot // rows) * 8, 8), 8)

    def advance_member(c, ml):
        m = c * CHUNK + ml

        def from_wide(i, f):
            return inside(wide[m, i, f], i, HALO)

        for i, f, value in stage(from_wide, None, rows + 4, 0.0, 1.0):
            mid[i, f] = inside(value, i, 2)
        for i, f, value in stage(lambda i, f: mid[i, f], lambda i, f: from_wide(i + 2, f), rows + 2, 0.75, 0.25):
            mid2[i, f] = inside(value, i, 1)
        result = {}
        for i, f, value in stage(lambda i, f: mid2[i, f], lambda i, f: wide[m, i + 3, f], rows, 1.0 / 3.0, 2.0 / 3.0):
            result[i, f] = value
        for f in range(fields):
            pieces = [result[r, f] for r in range(rows)]
            for q in range(rows):
                packed[c, q, f // held, pl.ds(ml * held + f % held, 8, stride=8), :] = choose(pieces, q)

    mine, others = pl.ds(pl.multiple_of(me * 8, 8), 8), pl.ds(0, (n_mem - 1) * 8)
    my_q, my_rows = position(me)

    def peer_of(i):
        return lax.rem(me + 1 + lax.rem(i + n_mem // 2 - 1, n_mem - 1), n_mem)

    def chunk_step(c, _):
        @pl.when(has_south)
        def _():
            upward(c).wait_recv()

        @pl.when(has_north)
        def _():
            downward(c).wait_recv()

        for ml in range(CHUNK):
            advance_member(c, ml)

        def send(i, _):
            peer = peer_of(i)
            q, place = position(peer)
            pltpu.make_async_remote_copy(
                src_ref=packed.at[c, q, :, place], dst_ref=gathered.at[c, :, mine],
                send_sem=send_a.at[c], recv_sem=recv_a.at[c],
                device_id={"mem": peer}, device_id_type=MESH,
            ).start()
            return 0

        lax.fori_loop(0, n_mem - 1, send, 0)
        gathered[c, :, mine] = packed[c, my_q, :, my_rows]
        return 0

    lax.fori_loop(0, chunks, chunk_step, 0)

    for c in range(chunks):
        pltpu.make_async_copy(gathered.at[c, :, others], gathered.at[c, :, others], recv_a.at[c]).wait()

    total = n_mem * members
    values_all = jnp.concatenate(
        [
            jnp.concatenate(
                [gathered[c, f // held, pl.ds(f % held, n_mem * CHUNK, stride=held), :] for f in range(fields)],
                axis=1,
            )
            for c in range(chunks)
        ],
        axis=0,
    )
    cells = values_all.shape[1]
    xbar = jnp.sum(values_all, axis=0, keepdims=True) * (1.0 / total)
    pert = values_all - xbar
    nobs = values_ref.shape[1]
    eye = (
        lax.broadcasted_iota(jnp.int32, (nobs, nobs), 0)
        == lax.broadcasted_iota(jnp.int32, (nobs, nobs), 1)
    )
    cell = cell_ref[...].astype(jnp.float32)
    cell_col = jnp.sum(jnp.where(eye, cell, 0.0), axis=1, keepdims=True).astype(jnp.int32)
    onehot = jnp.where(lax.broadcasted_iota(jnp.int32, (nobs, cells), 1) == cell_col, 1.0, 0.0)
    ypt = mm(onehot, pert, ((1,), (1,)))
    yp = mm(pert, onehot, ((1,), (1,)))
    kept, on_obs, common = analysis_weights(
        ypt, pert, onehot, xbar, values_ref[...], variance_ref[...],
        loop_ref[...].astype(jnp.float32), count_ref[...], float(total),
    )
    updated = kept * pert + mm(yp, on_obs) + common
    size = n_mem * CHUNK
    for c in range(chunks):
        for f in range(fields):
            fresh[c, f // held, pl.ds(f % held, size, stride=held), :] = updated[
                c * size : (c + 1) * size, f * 128 : (f + 1) * 128
            ]

    def send_back(i, _):
        peer = peer_of(i)
        place = pl.ds(pl.multiple_of(peer * 8, 8), 8)
        pltpu.make_async_remote_copy(
            src_ref=fresh.at[:, :, place], dst_ref=back.at[:, my_q, :, my_rows],
            send_sem=send_b, recv_sem=recv_b,
            device_id={"mem": peer}, device_id_type=MESH,
        ).start()
        return 0

    lax.fori_loop(0, n_mem - 1, send_back, 0)
    back[:, my_q, :, my_rows] = fresh[:, :, mine]

    for c in range(chunks):
        pltpu.make_async_copy(gathered.at[c, :, others], gathered.at[c, :, others], send_a.at[c]).wait()

    @pl.when(has_north)
    def _():
        for c in range(chunks):
            upward(c).wait_send()

    @pl.when(has_south)
    def _():
        for c in range(chunks):
            downward(c).wait_send()

    everyone = fresh.at[:, :, others]
    pltpu.make_async_copy(everyone, everyone, recv_b).wait()

    for m in range(members):
        c, ml = m // CHUNK, m % CHUNK
        for f in range(fields):
            pieces = [back[c, q, f // held, pl.ds(ml * held + f % held, 8, stride=8), :] for q in range(rows)]
            for r in range(rows):
                o_ref[m, f, pl.ds(r, 8, stride=rows), :] = choose(pieces, r)

    pltpu.make_async_copy(everyone, everyone, send_b).wait()


def per_device(ensemble, obs_value, obs_var, obs_cell, obs_loop, obs_count):
    members, fields, rows, width = ensemble.shape
    n_mem = lax.axis_size("mem")
    f32 = jnp.float32
    vmem = pl.BlockSpec(memory_space=pltpu.VMEM)
    blocks = width // 128
    chunks = members // CHUNK
    spans = fields * CHUNK // 8
    view = (
        ensemble.reshape(members, fields, rows, blocks, 128)
        .transpose(0, 1, 3, 2, 4)
        .reshape(members, fields, blocks * rows, 128)
    )
    out = pl.pallas_call(
        kernel,
        out_shape=jax.ShapeDtypeStruct(view.shape, f32),
        in_specs=[vmem] * 6,
        out_specs=vmem,
        scratch_shapes=[
            pltpu.VMEM((members, rows + 2 * HALO, fields, 8, 128), f32),
            pltpu.VMEM((rows + 4, fields, 8, 128), f32),
            pltpu.VMEM((rows + 2, fields, 8, 128), f32),
            pltpu.VMEM((chunks, rows, spans, 64, 128), f32),
            pltpu.VMEM((chunks, spans, n_mem * 8, 128), f32),
            pltpu.VMEM((chunks, spans, n_mem * 8, 128), f32),
            pltpu.VMEM((chunks, rows, spans, 64, 128), f32),
            pltpu.SemaphoreType.DMA((2, chunks)),
            pltpu.SemaphoreType.DMA((2, chunks)),
            pltpu.SemaphoreType.DMA((chunks,)),
            pltpu.SemaphoreType.DMA((chunks,)),
            pltpu.SemaphoreType.DMA,
            pltpu.SemaphoreType.DMA,
        ],
        compiler_params=pltpu.CompilerParams(collective_id=0, has_side_effects=True),
    )(
        view, obs_value[0], obs_var[0], obs_cell[0], obs_loop[0], obs_count,
    )
    return (
        out.reshape(members, fields, blocks, rows, 128)
        .transpose(0, 1, 3, 2, 4)
        .reshape(ensemble.shape)
    )


def solution(mesh):
    placed = (
        P("mem", None, "lat", None),
        P(None, ("mem", "lat"), None),
        P(None, ("mem", "lat"), None),
        P(None, ("mem", "lat"), None),
        P(None, ("mem", "lat"), None),
        P(None, ("mem", "lat")),
    )
    return jax.shard_map(
        per_device,
        mesh=mesh,
        in_specs=placed,
        out_specs=P("mem", None, "lat", None),
        check_vma=False,
    )
```

```python
import jax
import jax.numpy as jnp
from jax import lax
from jax.experimental import pallas as pl
from jax.experimental.pallas import tpu as pltpu
from jax.sharding import PartitionSpec as P

MESH = pl.DeviceIdType.MESH
NSI = 5
DT = 0.15
VISC = 0.1
CHUNK = 2
HALO = 3


def choose(pieces, offset, quarter):
    out = None
    for r, piece in enumerate(pieces):
        turned = pltpu.roll(piece, ((r - offset) * 32) % 128, 1) if r != offset else piece
        out = turned if out is None else jnp.where(quarter == r, turned, out)
    return out


def split(x):
    high = x.astype(jnp.bfloat16)
    return high, (x - high.astype(jnp.float32)).astype(jnp.bfloat16)


def dot(a, b, dims=((1,), (0,))):
    return lax.dot_general(a, b, (dims, ((), ())), preferred_element_type=jnp.float32)


def mm(a, b, dims=((1,), (0,))):
    return dot(a[0], b[0], dims) + (dot(a[0], b[1], dims) + dot(a[1], b[0], dims))


def product(a, b):
    terms = [a[:, k : k + 1] * b[k : k + 1, :] for k in range(a.shape[1])]
    while len(terms) > 1:
        terms = [x + y for x, y in zip(terms[::2], terms[1::2])]
    return terms[0]


def diagonal_of(size):
    return lax.broadcasted_iota(jnp.int32, (size, size), 0) == lax.broadcasted_iota(
        jnp.int32, (size, size), 1
    )


def as_column(row, eye):
    return jnp.sum(jnp.where(eye, row, 0.0), axis=1, keepdims=True)


def as_row(column, eye):
    return jnp.sum(jnp.where(eye, column, 0.0), axis=0, keepdims=True)


def solve(gram, innovation, weight, eye, members):
    nobs = gram.shape[0]
    weight_col = as_column(weight, eye)
    trace = jnp.sum(jnp.where(eye, gram * weight, 0.0), axis=(0, 1), keepdims=True)
    inverse = 1.0 / (members - 1.0 + 0.5 * trace)
    a = (members - 1.0) * inverse
    t = gram * (weight * inverse)
    identity = jnp.where(eye, 1.0, 0.0)
    group = lax.broadcasted_iota(jnp.int32, (nobs, 4 * nobs), 1) // nobs
    state = jnp.concatenate([a * identity + t, identity, identity, jnp.zeros_like(t)], axis=1)
    p0, z0 = a, jnp.ones_like(a)
    for repeat in range(NSI):
        g0 = 1.5 - 0.5 * p0
        g = 1.5 * identity - 0.5 * state[:, :nobs]
        h = state[:, nobs : 2 * nobs]
        spread_h = jnp.concatenate([h, h, h, h], axis=1)
        along = jnp.where(group == 1, -0.5 * p0, jnp.where(group == 3, -0.5 * z0, 0.0))
        state = product(g, state) + along * spread_h
        z0 = z0 * g0
        if repeat < NSI - 1:
            again = product(g, state) + jnp.where(group == 1, -0.5 * p0 * g0, 0.0) * spread_h
            state = jnp.where(group < 2, again, state)
            p0 = p0 * g0 * g0
    z = state[:, 2 * nobs : 3 * nobs]
    root = jnp.sqrt(a)
    shift = weight_col * product(z, product(z, innovation)) * inverse
    return root * z0, (root * inverse) * weight_col * state[:, 3 * nobs :], shift


def kernel(
    x_ref, values_ref, variance_ref, cell_ref, loop_ref, count_ref, o_ref,
    wide, mid, mid2, packed, gathered, fresh, centred,
    halo_send, halo_recv, send_a, recv_a, send_b, recv_b, own_b,
):
    n_mem, n_lat = lax.axis_size("mem"), lax.axis_size("lat")
    me, band = lax.axis_index("mem"), lax.axis_index("lat")
    members, fields, _, _ = x_ref.shape
    rows = 4
    chunks = members // CHUNK
    spans = packed.shape[2]
    held = fields // spans

    barrier = pltpu.get_barrier_semaphore()

    def greet(k, _):
        pl.semaphore_signal(
            barrier, inc=1, device_id={"mem": lax.rem(me + k, n_mem)}, device_id_type=MESH
        )
        return 0

    @pl.when(band < n_lat - 1)
    def _():
        pl.semaphore_signal(barrier, inc=1, device_id={"lat": band + 1}, device_id_type=MESH)

    @pl.when(band > 0)
    def _():
        pl.semaphore_signal(barrier, inc=1, device_id={"lat": band - 1}, device_id_type=MESH)

    lax.fori_loop(1, n_mem, greet, 0)

    def spread_rows(m, _):
        for f in range(fields):
            for r in range(rows):
                wide[m, HALO + r, f] = x_ref[m, f, pl.ds(r, 8, stride=rows), :]
        return 0

    lax.fori_loop(0, members, spread_rows, 0)

    beside = (band + n_lat - 1) // n_lat + (2 * n_lat - 2 - band) // n_lat
    pl.semaphore_wait(barrier, n_mem - 1 + beside)

    def upward(c):
        part = pl.ds(c * CHUNK, CHUNK)
        return pltpu.make_async_remote_copy(
            src_ref=wide.at[part, pl.ds(rows, HALO)], dst_ref=wide.at[part, pl.ds(0, HALO)],
            send_sem=halo_send.at[0, c], recv_sem=halo_recv.at[0, c],
            device_id={"lat": band + 1}, device_id_type=MESH,
        )

    def downward(c):
        part = pl.ds(c * CHUNK, CHUNK)
        return pltpu.make_async_remote_copy(
            src_ref=wide.at[part, pl.ds(HALO, HALO)], dst_ref=wide.at[part, pl.ds(HALO + rows, HALO)],
            send_sem=halo_send.at[1, c], recv_sem=halo_recv.at[1, c],
            device_id={"lat": band - 1}, device_id_type=MESH,
        )

    @pl.when(band < n_lat - 1)
    def _():
        for c in range(chunks):
            upward(c).start()

    @pl.when(band > 0)
    def _():
        for c in range(chunks):
            downward(c).start()

    lane = lax.broadcasted_iota(jnp.int32, (8, 128), 1)
    last_lane, first_lane = lane == 127, lane == 0
    quarter = lane // 32
    has_south, has_north = band > 0, band < n_lat - 1

    def east(c):
        turned = pltpu.roll(c, 127, 1)
        return jnp.where(last_lane, pltpu.roll(turned, 7, 0), turned)

    def west(c):
        turned = pltpu.roll(c, 1, 1)
        return jnp.where(first_lane, pltpu.roll(turned, 1, 0), turned)

    def stage(source, base, count, weight_base, weight_mid):
        scale = weight_mid * DT
        for i in range(count):
            u = 0.5 * scale * source(i + 1, 0)
            v = 0.5 * scale * source(i + 1, 1)
            drag = scale * VISC
            east_w, west_w, north_w, south_w = drag - u, drag + u, drag - v, drag + v
            for f in range(fields):
                c = source(i + 1, f)
                total = (weight_mid - 4.0 * drag) * c
                total += north_w * source(i + 2, f) + south_w * source(i, f)
                total += east_w * east(c) + west_w * west(c)
                if weight_base:
                    total += weight_base * base(i, f)
                yield i, f, total

    def inside(value, i, extra):
        if i < extra:
            return jnp.where(has_south, value, 0.0)
        if i >= extra + rows:
            return jnp.where(has_north, value, 0.0)
        return value

    def position(slot):
        return lax.rem(slot, rows), pl.ds(pl.multiple_of((slot // rows) * 8, 8), 8)

    def advance_member(c, ml):
        m = c * CHUNK + ml

        def from_wide(i, f):
            return inside(wide[m, i, f], i, HALO)

        for i, f, value in stage(from_wide, None, rows + 4, 0.0, 1.0):
            mid[i, f] = inside(value, i, 2)
        for i, f, value in stage(lambda i, f: mid[i, f], lambda i, f: from_wide(i + 2, f), rows + 2, 0.75, 0.25):
            mid2[i, f] = inside(value, i, 1)
        result = {}
        for i, f, value in stage(lambda i, f: mid2[i, f], lambda i, f: wide[m, i + 3, f], rows, 1.0 / 3.0, 2.0 / 3.0):
            result[i, f] = value
        for f in range(fields):
            pieces = [result[r, f] for r in range(rows)]
            for q in range(rows):
                packed[c, q, f // held, pl.ds(ml * held + f % held, 8, stride=8), :] = choose(pieces, q, quarter)

    mine, others = pl.ds(pl.multiple_of(me * 8, 8), 8), pl.ds(0, (n_mem - 1) * 8)
    my_q, my_rows = position(me)

    def peer_of(i):
        step, kind = i // 4, lax.rem(i, 4)
        odd = lax.rem(step, 2)
        dy = n_mem // 8 + (step // 2) * (1 - odd) - ((step + 1) // 2) * odd
        y = lax.rem(me // 4 + dy, n_mem // 4)
        x = lax.rem(lax.rem(me, 4) // 2 + 1 - kind // 2, 2)
        core = lax.rem(lax.rem(me, 2) + 1 - lax.rem(kind, 2), 2)
        return y * 4 + x * 2 + core

    def chunk_step(c, _):
        @pl.when(has_south)
        def _():
            upward(c).wait_recv()

        @pl.when(has_north)
        def _():
            downward(c).wait_recv()

        for ml in range(CHUNK):
            advance_member(c, ml)

        def send(i, _):
            peer = peer_of(i)
            q, place = position(peer)
            pltpu.make_async_remote_copy(
                src_ref=packed.at[c, q, :, place], dst_ref=gathered.at[c, :, mine],
                send_sem=send_a.at[c], recv_sem=recv_a.at[c],
                device_id={"mem": peer}, device_id_type=MESH,
            ).start()
            return 0

        lax.fori_loop(0, n_mem - 1, send, 0)
        gathered[c, :, mine] = packed[c, my_q, :, my_rows]
        return 0

    lax.fori_loop(0, chunks, chunk_step, 0)

    nobs = values_ref.shape[1]
    eye = diagonal_of(nobs)
    cells = fields * 128
    cell_col = as_column(cell_ref[...].astype(jnp.float32), eye).astype(jnp.int32)
    is_cell = lax.broadcasted_iota(jnp.int32, (nobs, cells), 1) == cell_col
    onehot = jnp.where(is_cell, 1.0, 0.0)
    pick = onehot.astype(jnp.bfloat16)
    slots = lax.broadcasted_iota(jnp.int32, (1, nobs), 1)
    decay = jnp.exp(-0.35 * loop_ref[...].astype(jnp.float32)) / variance_ref[...]
    weight = jnp.where(slots < count_ref[...], decay, 0.0)

    total = n_mem * members
    size = n_mem * CHUNK
    seen_parts = []
    for c in range(chunks):
        pltpu.make_async_copy(gathered.at[c, :, others], gathered.at[c, :, others], recv_a.at[c]).wait()
        block = jnp.concatenate(
            [gathered[c, f // held, pl.ds(f % held, size, stride=held), :] for f in range(fields)], axis=1
        )
        if c == 0:
            origin = jnp.sum(block, axis=0, keepdims=True) * (1.0 / size)
        moved = block - origin
        centred[c] = moved
        parts = split(moved)
        seen = dot(parts[0], pick, ((1,), (1,))) + dot(parts[1], pick, ((1,), (1,)))
        seen_t = dot(pick, parts[0], ((1,), (1,))) + dot(pick, parts[1], ((1,), (1,)))
        turned = split(seen_t)
        seen_parts.append(split(seen))
        cross_c = mm(turned, parts)
        gram_c = mm(turned, turned, ((1,), (1,)))
        sum_c = jnp.sum(moved, axis=0, keepdims=True)
        if c == 0:
            cross, gram, summed = cross_c, gram_c, sum_c
        else:
            cross, gram, summed = cross + cross_c, gram + gram_c, summed + sum_c

    offset = summed * (1.0 / total)
    offset_seen = jnp.sum(onehot * offset, axis=1, keepdims=True)
    origin_seen = jnp.sum(onehot * origin, axis=1, keepdims=True)
    cross = cross - (float(total) * offset_seen) * offset
    gram = gram - (float(total) * offset_seen) * as_row(offset_seen, eye)
    innovation = as_column(values_ref[...], eye) - (origin_seen + offset_seen)
    kept, on_cross, shift = solve(gram, innovation, weight, eye, float(total))
    rows_seen = product(on_cross, cross)
    common = (
        origin + (1.0 - kept) * offset
        + jnp.sum(shift * cross - offset_seen * rows_seen, axis=0, keepdims=True)
    )
    rows_parts = split(rows_seen)
    for c in range(chunks):
        updated = kept * centred[c] + (mm(seen_parts[c], rows_parts) + common)
        for f in range(fields):
            fresh[c, f // held, pl.ds(f % held, size, stride=held), :] = updated[:, f * 128 : (f + 1) * 128]

        def send_back(i, _):
            peer = peer_of(i)
            place = pl.ds(pl.multiple_of(peer * 8, 8), 8)
            pltpu.make_async_remote_copy(
                src_ref=fresh.at[c, :, place], dst_ref=o_ref.at[c, my_q, :, my_rows],
                send_sem=send_b.at[c], recv_sem=recv_b.at[c],
                device_id={"mem": peer}, device_id_type=MESH,
            ).start()
            return 0

        lax.fori_loop(0, n_mem - 1, send_back, 0)
    own = pltpu.make_async_copy(fresh.at[:, :, mine], o_ref.at[:, my_q, :, my_rows], own_b)
    own.start()

    for c in range(chunks):
        pltpu.make_async_copy(gathered.at[c, :, others], gathered.at[c, :, others], send_a.at[c]).wait()

    @pl.when(has_north)
    def _():
        for c in range(chunks):
            upward(c).wait_send()

    @pl.when(has_south)
    def _():
        for c in range(chunks):
            downward(c).wait_send()

    own.wait()
    for c in range(chunks):
        pltpu.make_async_copy(fresh.at[c, :, others], fresh.at[c, :, others], send_b.at[c]).wait()
        pltpu.make_async_copy(fresh.at[c, :, others], fresh.at[c, :, others], recv_b.at[c]).wait()


def unpack_kernel(back_ref, o_ref):
    rows, spans = back_ref.shape[1], back_ref.shape[2]
    fields = o_ref.shape[1]
    held = fields // spans
    quarter = lax.broadcasted_iota(jnp.int32, (8, 128), 1) // 32
    for ml in range(CHUNK):
        for f in range(fields):
            pieces = [back_ref[0, q, f // held, pl.ds(ml * held + f % held, 8, stride=8), :] for q in range(rows)]
            for r in range(rows):
                o_ref[ml, f, pl.ds(r, 8, stride=rows), :] = choose(pieces, r, quarter)


def per_device(ensemble, obs_value, obs_var, obs_cell, obs_loop, obs_count):
    members, fields, rows, width = ensemble.shape
    n_mem = lax.axis_size("mem")
    f32 = jnp.float32
    vmem = pl.BlockSpec(memory_space=pltpu.VMEM)
    blocks = width // 128
    chunks = members // CHUNK
    spans = fields * CHUNK // 8
    view = (
        ensemble.reshape(members, fields, rows, blocks, 128)
        .transpose(0, 1, 3, 2, 4)
        .reshape(members, fields, blocks * rows, 128)
    )
    back = pl.pallas_call(
        kernel,
        out_shape=jax.ShapeDtypeStruct((chunks, rows, spans, 64, 128), f32),
        in_specs=[vmem] * 6,
        out_specs=pl.BlockSpec(memory_space=pl.ANY),
        scratch_shapes=[
            pltpu.VMEM((members, rows + 2 * HALO, fields, 8, 128), f32),
            pltpu.VMEM((rows + 4, fields, 8, 128), f32),
            pltpu.VMEM((rows + 2, fields, 8, 128), f32),
            pltpu.VMEM((chunks, rows, spans, 64, 128), f32),
            pltpu.VMEM((chunks, spans, n_mem * 8, 128), f32),
            pltpu.VMEM((chunks, spans, n_mem * 8, 128), f32),
            pltpu.VMEM((chunks, n_mem * CHUNK, fields * 128), f32),
            pltpu.SemaphoreType.DMA((2, chunks)),
            pltpu.SemaphoreType.DMA((2, chunks)),
            pltpu.SemaphoreType.DMA((chunks,)),
            pltpu.SemaphoreType.DMA((chunks,)),
            pltpu.SemaphoreType.DMA((chunks,)),
            pltpu.SemaphoreType.DMA((chunks,)),
            pltpu.SemaphoreType.DMA,
        ],
        compiler_params=pltpu.CompilerParams(collective_id=0, has_side_effects=True),
    )(
        view, obs_value[0], obs_var[0], obs_cell[0], obs_loop[0], obs_count,
    )
    out = pl.pallas_call(
        unpack_kernel,
        grid=(chunks,),
        out_shape=jax.ShapeDtypeStruct(view.shape, f32),
        in_specs=[pl.BlockSpec((1, rows, spans, 64, 128), lambda c: (c, 0, 0, 0, 0))],
        out_specs=pl.BlockSpec((CHUNK, fields, blocks * rows, 128), lambda c: (c, 0, 0, 0)),
    )(back)
    return (
        out.reshape(members, fields, blocks, rows, 128)
        .transpose(0, 1, 3, 2, 4)
        .reshape(ensemble.shape)
    )


def solution(mesh):
    placed = (
        P("mem", None, "lat", None),
        P(None, ("mem", "lat"), None),
        P(None, ("mem", "lat"), None),
        P(None, ("mem", "lat"), None),
        P(None, ("mem", "lat"), None),
        P(None, ("mem", "lat")),
    )
    return jax.shard_map(
        per_device,
        mesh=mesh,
        in_specs=placed,
        out_specs=P("mem", None, "lat", None),
        check_vma=False,
    )
```

```python
import jax
import jax.numpy as jnp
from jax import lax
from jax.experimental import pallas as pl
from jax.experimental.pallas import tpu as pltpu
from jax.sharding import PartitionSpec as P

MESH = pl.DeviceIdType.MESH
NSI = 5
DT = 0.15
VISC = 0.1
CHUNK = 2
HALO = 3


def choose(pieces, offset, quarter):
    out = None
    for r, piece in enumerate(pieces):
        turned = pltpu.roll(piece, ((r - offset) * 32) % 128, 1) if r != offset else piece
        out = turned if out is None else jnp.where(quarter == r, turned, out)
    return out


def split(x):
    high = x.astype(jnp.bfloat16)
    return high, (x - high.astype(jnp.float32)).astype(jnp.bfloat16)


def dot(a, b, dims=((1,), (0,))):
    return lax.dot_general(a, b, (dims, ((), ())), preferred_element_type=jnp.float32)


def mm(a, b, dims=((1,), (0,))):
    return dot(a[0], b[0], dims) + (dot(a[0], b[1], dims) + dot(a[1], b[0], dims))


def product(a, b):
    terms = [a[:, k : k + 1] * b[k : k + 1, :] for k in range(a.shape[1])]
    while len(terms) > 1:
        terms = [x + y for x, y in zip(terms[::2], terms[1::2])]
    return terms[0]


def diagonal_of(size):
    return lax.broadcasted_iota(jnp.int32, (size, size), 0) == lax.broadcasted_iota(
        jnp.int32, (size, size), 1
    )


def as_column(row, eye):
    return jnp.sum(jnp.where(eye, row, 0.0), axis=1, keepdims=True)


def as_row(column, eye):
    return jnp.sum(jnp.where(eye, column, 0.0), axis=0, keepdims=True)


def solve(gram, innovation, weight, eye, members):
    nobs = gram.shape[0]
    weight_col = as_column(weight, eye)
    trace = jnp.sum(jnp.where(eye, gram * weight, 0.0), axis=(0, 1), keepdims=True)
    inverse = 1.0 / (members - 1.0 + 0.5 * trace)
    a = (members - 1.0) * inverse
    t = gram * (weight * inverse)
    identity = jnp.where(eye, 1.0, 0.0)
    group = lax.broadcasted_iota(jnp.int32, (nobs, 4 * nobs), 1) // nobs
    state = jnp.concatenate([a * identity + t, identity, identity, jnp.zeros_like(t)], axis=1)
    p0, z0 = a, jnp.ones_like(a)
    for repeat in range(NSI):
        g0 = 1.5 - 0.5 * p0
        g = 1.5 * identity - 0.5 * state[:, :nobs]
        h = state[:, nobs : 2 * nobs]
        spread_h = jnp.concatenate([h, h, h, h], axis=1)
        along = jnp.where(group == 1, -0.5 * p0, jnp.where(group == 3, -0.5 * z0, 0.0))
        state = product(g, state) + along * spread_h
        z0 = z0 * g0
        if repeat < NSI - 1:
            again = product(g, state) + jnp.where(group == 1, -0.5 * p0 * g0, 0.0) * spread_h
            state = jnp.where(group < 2, again, state)
            p0 = p0 * g0 * g0
    z = state[:, 2 * nobs : 3 * nobs]
    root = jnp.sqrt(a)
    shift = weight_col * product(z, product(z, innovation)) * inverse
    return root * z0, (root * inverse) * weight_col * state[:, 3 * nobs :], shift


def kernel(
    x_hbm, values_hbm, variance_hbm, cell_hbm, loop_hbm, count_hbm, o_ref,
    x_ref, values_ref, variance_ref, cell_ref, loop_ref, count_ref, wide, mid, mid2, packed, gathered, fresh, centred,
    halo_send, halo_recv, send_a, recv_a, send_b, recv_b, own_b, load_x, load_small,
):
    n_mem, n_lat = lax.axis_size("mem"), lax.axis_size("lat")
    me, band = lax.axis_index("mem"), lax.axis_index("lat")
    members, fields, _, _ = x_hbm.shape
    rows = 4
    chunks = members // CHUNK
    spans = packed.shape[2]
    held = fields // spans

    loads = [
        pltpu.make_async_copy(
            x_hbm.at[pl.ds(c * CHUNK, CHUNK)], x_ref.at[pl.ds(c * CHUNK, CHUNK)], load_x.at[c]
        )
        for c in range(chunks)
    ]
    small = [
        pltpu.make_async_copy(source, target, load_small.at[k])
        for k, (source, target) in enumerate(
            (
                (values_hbm, values_ref), (variance_hbm, variance_ref), (cell_hbm, cell_ref),
                (loop_hbm, loop_ref), (count_hbm, count_ref),
            )
        )
    ]
    for load in loads + small:
        load.start()

    ring = n_mem // 4
    my_y = me // 4
    my_x = (me - 4 * my_y) // 2
    my_core = me - 4 * my_y - 2 * my_x
    ys = [my_y] + [jnp.where(my_y + k >= ring, my_y + k - ring, my_y + k) for k in range(1, ring)]
    xs = (my_x, 1 - my_x)
    cores = (my_core, 1 - my_core)
    order = [ring // 2]
    for k in range(1, ring // 2):
        order += [ring // 2 - k, ring // 2 + k]
    peers = [
        (ys[k], 2 * xs[x] + cores[core])
        for k in order + [0]
        for x, core in ((1, 1), (1, 0), (0, 1), (0, 0))
        if k or x or core
    ]

    barrier = pltpu.get_barrier_semaphore()

    @pl.when(band < n_lat - 1)
    def _():
        pl.semaphore_signal(barrier, inc=1, device_id={"lat": band + 1}, device_id_type=MESH)

    @pl.when(band > 0)
    def _():
        pl.semaphore_signal(barrier, inc=1, device_id={"lat": band - 1}, device_id_type=MESH)

    for y, q in peers:
        pl.semaphore_signal(barrier, inc=1, device_id={"mem": 4 * y + q}, device_id_type=MESH)

    def spread_rows(c):
        loads[c].wait()
        for m in range(c * CHUNK, (c + 1) * CHUNK):
            for f in range(fields):
                for r in range(rows):
                    wide[m, HALO + r, f] = x_ref[m, f, pl.ds(r, 8, stride=rows), :]

    spread_rows(0)
    beside = (band + n_lat - 1) // n_lat + (2 * n_lat - 2 - band) // n_lat
    pl.semaphore_wait(barrier, n_mem - 1 + beside)

    def upward(c):
        part = pl.ds(c * CHUNK, CHUNK)
        return pltpu.make_async_remote_copy(
            src_ref=wide.at[part, pl.ds(rows, HALO)], dst_ref=wide.at[part, pl.ds(0, HALO)],
            send_sem=halo_send.at[0, c], recv_sem=halo_recv.at[0, c],
            device_id={"lat": band + 1}, device_id_type=MESH,
        )

    def downward(c):
        part = pl.ds(c * CHUNK, CHUNK)
        return pltpu.make_async_remote_copy(
            src_ref=wide.at[part, pl.ds(HALO, HALO)], dst_ref=wide.at[part, pl.ds(HALO + rows, HALO)],
            send_sem=halo_send.at[1, c], recv_sem=halo_recv.at[1, c],
            device_id={"lat": band - 1}, device_id_type=MESH,
        )

    for c in range(chunks):
        if c:
            spread_rows(c)

        @pl.when(band < n_lat - 1)
        def _():
            upward(c).start()

        @pl.when(band > 0)
        def _():
            downward(c).start()

    lane = lax.broadcasted_iota(jnp.int32, (8, 128), 1)
    last_lane, first_lane = lane == 127, lane == 0
    quarter = lane // 32
    has_south, has_north = band > 0, band < n_lat - 1

    def east(c):
        turned = pltpu.roll(c, 127, 1)
        return jnp.where(last_lane, pltpu.roll(turned, 7, 0), turned)

    def west(c):
        turned = pltpu.roll(c, 1, 1)
        return jnp.where(first_lane, pltpu.roll(turned, 1, 0), turned)

    def stage(source, base, count, weight_base, weight_mid):
        scale = weight_mid * DT
        for i in range(count):
            u = 0.5 * scale * source(i + 1, 0)
            v = 0.5 * scale * source(i + 1, 1)
            drag = scale * VISC
            east_w, west_w, north_w, south_w = drag - u, drag + u, drag - v, drag + v
            for f in range(fields):
                c = source(i + 1, f)
                total = (weight_mid - 4.0 * drag) * c
                total += north_w * source(i + 2, f) + south_w * source(i, f)
                total += east_w * east(c) + west_w * west(c)
                if weight_base:
                    total += weight_base * base(i, f)
                yield i, f, total

    def inside(value, i, extra):
        if i < extra:
            return jnp.where(has_south, value, 0.0)
        if i >= extra + rows:
            return jnp.where(has_north, value, 0.0)
        return value

    def advance_member(c, ml):
        m = c * CHUNK + ml

        def from_wide(i, f):
            return inside(wide[m, i, f], i, HALO)

        for i, f, value in stage(from_wide, None, rows + 4, 0.0, 1.0):
            mid[i, f] = inside(value, i, 2)
        for i, f, value in stage(lambda i, f: mid[i, f], lambda i, f: from_wide(i + 2, f), rows + 2, 0.75, 0.25):
            mid2[i, f] = inside(value, i, 1)
        result = {}
        for i, f, value in stage(lambda i, f: mid2[i, f], lambda i, f: wide[m, i + 3, f], rows, 1.0 / 3.0, 2.0 / 3.0):
            result[i, f] = value
        for f in range(fields):
            pieces = [result[r, f] for r in range(rows)]
            for q in range(rows):
                packed[c, q, f // held, pl.ds(ml * held + f % held, 8, stride=8), :] = choose(pieces, q, quarter)

    mine, others = pl.ds(pl.multiple_of(me * 8, 8), 8), pl.ds(0, (n_mem - 1) * 8)
    my_q, my_rows = me - 4 * my_y, pl.ds(pl.multiple_of(my_y * 8, 8), 8)

    def chunk_step(c, _):
        @pl.when(has_south)
        def _():
            upward(c).wait_recv()

        @pl.when(has_north)
        def _():
            downward(c).wait_recv()

        for ml in range(CHUNK):
            advance_member(c, ml)

        for y, q in peers:
            pltpu.make_async_remote_copy(
                src_ref=packed.at[c, q, :, pl.ds(pl.multiple_of(y * 8, 8), 8)], dst_ref=gathered.at[c, :, mine],
                send_sem=send_a.at[c], recv_sem=recv_a.at[c],
                device_id={"mem": 4 * y + q}, device_id_type=MESH,
            ).start()

        gathered[c, :, mine] = packed[c, my_q, :, my_rows]
        return 0

    lax.fori_loop(0, chunks, chunk_step, 0)

    for load in small:
        load.wait()
    nobs = values_ref.shape[1]
    eye = diagonal_of(nobs)
    cells = fields * 128
    cell_col = as_column(cell_ref[...].astype(jnp.float32), eye).astype(jnp.int32)
    is_cell = lax.broadcasted_iota(jnp.int32, (nobs, cells), 1) == cell_col
    onehot = jnp.where(is_cell, 1.0, 0.0)
    pick = onehot.astype(jnp.bfloat16)
    slots = lax.broadcasted_iota(jnp.int32, (1, nobs), 1)
    decay = jnp.exp(-0.35 * loop_ref[...].astype(jnp.float32)) / variance_ref[...]
    weight = jnp.where(slots < count_ref[...], decay, 0.0)

    total = n_mem * members
    size = n_mem * CHUNK
    seen_parts = []
    for c in range(chunks):
        pltpu.make_async_copy(gathered.at[c, :, others], gathered.at[c, :, others], recv_a.at[c]).wait()
        block = jnp.concatenate(
            [gathered[c, f // held, pl.ds(f % held, size, stride=held), :] for f in range(fields)], axis=1
        )
        if c == 0:
            origin = jnp.sum(block, axis=0, keepdims=True) * (1.0 / size)
        moved = block - origin
        centred[c] = moved
        parts = split(moved)
        seen = dot(parts[0], pick, ((1,), (1,))) + dot(parts[1], pick, ((1,), (1,)))
        seen_t = dot(pick, parts[0], ((1,), (1,))) + dot(pick, parts[1], ((1,), (1,)))
        turned = split(seen_t)
        seen_parts.append(split(seen))
        cross_c = mm(turned, parts)
        gram_c = mm(turned, turned, ((1,), (1,)))
        sum_c = jnp.sum(moved, axis=0, keepdims=True)
        if c == 0:
            cross, gram, summed = cross_c, gram_c, sum_c
        else:
            cross, gram, summed = cross + cross_c, gram + gram_c, summed + sum_c

    offset = summed * (1.0 / total)
    offset_seen = jnp.sum(onehot * offset, axis=1, keepdims=True)
    origin_seen = jnp.sum(onehot * origin, axis=1, keepdims=True)
    cross = cross - (float(total) * offset_seen) * offset
    gram = gram - (float(total) * offset_seen) * as_row(offset_seen, eye)
    innovation = as_column(values_ref[...], eye) - (origin_seen + offset_seen)
    kept, on_cross, shift = solve(gram, innovation, weight, eye, float(total))
    rows_seen = product(on_cross, cross)
    common = (
        origin + (1.0 - kept) * offset
        + jnp.sum(shift * cross - offset_seen * rows_seen, axis=0, keepdims=True)
    )
    rows_parts = split(rows_seen)
    for c in range(chunks):
        updated = kept * centred[c] + (mm(seen_parts[c], rows_parts) + common)
        for f in range(fields):
            fresh[c, f // held, pl.ds(f % held, size, stride=held), :] = updated[:, f * 128 : (f + 1) * 128]

        for y, q in peers:
            place = pl.ds(pl.multiple_of((4 * y + q) * 8, 8), 8)
            pltpu.make_async_remote_copy(
                src_ref=fresh.at[c, :, place], dst_ref=o_ref.at[c, my_q, :, my_rows],
                send_sem=send_b.at[c], recv_sem=recv_b.at[c],
                device_id={"mem": 4 * y + q}, device_id_type=MESH,
            ).start()

    own = pltpu.make_async_copy(fresh.at[:, :, mine], o_ref.at[:, my_q, :, my_rows], own_b)
    own.start()

    for c in range(chunks):
        pltpu.make_async_copy(gathered.at[c, :, others], gathered.at[c, :, others], send_a.at[c]).wait()

    @pl.when(has_north)
    def _():
        for c in range(chunks):
            upward(c).wait_send()

    @pl.when(has_south)
    def _():
        for c in range(chunks):
            downward(c).wait_send()

    own.wait()
    for c in range(chunks):
        pltpu.make_async_copy(fresh.at[c, :, others], fresh.at[c, :, others], send_b.at[c]).wait()
        pltpu.make_async_copy(fresh.at[c, :, others], fresh.at[c, :, others], recv_b.at[c]).wait()


def unpack_kernel(back_ref, o_hbm, o_ref, out_sem):
    chunks, rows, spans = back_ref.shape[:3]
    fields = o_ref.shape[1]
    held = fields // spans
    quarter = lax.broadcasted_iota(jnp.int32, (8, 128), 1) // 32
    stores = []
    for c in range(chunks):
        for ml in range(CHUNK):
            for f in range(fields):
                pieces = [back_ref[c, q, f // held, pl.ds(ml * held + f % held, 8, stride=8), :] for q in range(rows)]
                for r in range(rows):
                    o_ref[c * CHUNK + ml, f, pl.ds(r, 8, stride=rows), :] = choose(pieces, r, quarter)
        part = pl.ds(c * CHUNK, CHUNK)
        stores.append(pltpu.make_async_copy(o_ref.at[part], o_hbm.at[part], out_sem.at[c]))
        stores[-1].start()
    for store in stores:
        store.wait()


def per_device(ensemble, obs_value, obs_var, obs_cell, obs_loop, obs_count):
    members, fields, rows, width = ensemble.shape
    n_mem = lax.axis_size("mem")
    f32 = jnp.float32
    nobs = obs_value.shape[2]
    blocks = width // 128
    chunks = members // CHUNK
    spans = fields * CHUNK // 8
    view = (
        ensemble.reshape(members, fields, rows, blocks, 128)
        .transpose(0, 1, 3, 2, 4)
        .reshape(members, fields, blocks * rows, 128)
    )
    back = pl.pallas_call(
        kernel,
        out_shape=pltpu.VMEM((chunks, rows, spans, 64, 128), f32),
        in_specs=[pl.BlockSpec(memory_space=pl.ANY)] * 6,
        out_specs=pl.BlockSpec(memory_space=pltpu.VMEM),
        scratch_shapes=[
            pltpu.VMEM(view.shape, f32),
            pltpu.VMEM((1, nobs), f32),
            pltpu.VMEM((1, nobs), f32),
            pltpu.VMEM((1, nobs), jnp.int32),
            pltpu.VMEM((1, nobs), jnp.int32),
            pltpu.VMEM((1, 1), jnp.int32),
            pltpu.VMEM((members, rows + 2 * HALO, fields, 8, 128), f32),
            pltpu.VMEM((rows + 4, fields, 8, 128), f32),
            pltpu.VMEM((rows + 2, fields, 8, 128), f32),
            pltpu.VMEM((chunks, rows, spans, 64, 128), f32),
            pltpu.VMEM((chunks, spans, n_mem * 8, 128), f32),
            pltpu.VMEM((chunks, spans, n_mem * 8, 128), f32),
            pltpu.VMEM((chunks, n_mem * CHUNK, fields * 128), f32),
            pltpu.SemaphoreType.DMA((2, chunks)),
            pltpu.SemaphoreType.DMA((2, chunks)),
            pltpu.SemaphoreType.DMA((chunks,)),
            pltpu.SemaphoreType.DMA((chunks,)),
            pltpu.SemaphoreType.DMA((chunks,)),
            pltpu.SemaphoreType.DMA((chunks,)),
            pltpu.SemaphoreType.DMA,
            pltpu.SemaphoreType.DMA((chunks,)),
            pltpu.SemaphoreType.DMA((5,)),
        ],
        compiler_params=pltpu.CompilerParams(collective_id=0, has_side_effects=True),
    )(
        view, obs_value[0], obs_var[0], obs_cell[0], obs_loop[0], obs_count,
    )
    out = pl.pallas_call(
        unpack_kernel,
        out_shape=jax.ShapeDtypeStruct(view.shape, f32),
        in_specs=[pl.BlockSpec(memory_space=pltpu.VMEM)],
        out_specs=pl.BlockSpec(memory_space=pl.ANY),
        scratch_shapes=[pltpu.VMEM(view.shape, f32), pltpu.SemaphoreType.DMA((chunks,))],
    )(pltpu.with_memory_space_constraint(back, pltpu.VMEM))
    return (
        out.reshape(members, fields, blocks, rows, 128)
        .transpose(0, 1, 3, 2, 4)
        .reshape(ensemble.shape)
    )


def solution(mesh):
    placed = (
        P("mem", None, "lat", None),
        P(None, ("mem", "lat"), None),
        P(None, ("mem", "lat"), None),
        P(None, ("mem", "lat"), None),
        P(None, ("mem", "lat"), None),
        P(None, ("mem", "lat")),
    )
    return jax.shard_map(
        per_device,
        mesh=mesh,
        in_specs=placed,
        out_specs=P("mem", None, "lat", None),
        check_vma=False,
    )
```

```python
import jax
import jax.numpy as jnp
from jax import lax
from jax.experimental import pallas as pl
from jax.experimental.pallas import tpu as pltpu
from jax.sharding import PartitionSpec as P

MESH = pl.DeviceIdType.MESH
NSI = 5
DT = 0.15
VISC = 0.1
CHUNK = 2
HALO = 3


def choose(pieces, offset, quarter):
    out = None
    for r, piece in enumerate(pieces):
        turned = pltpu.roll(piece, ((r - offset) * 32) % 128, 1) if r != offset else piece
        out = turned if out is None else jnp.where(quarter == r, turned, out)
    return out


def split(x):
    high = x.astype(jnp.bfloat16)
    return high, (x - high.astype(jnp.float32)).astype(jnp.bfloat16)


def dot(a, b, dims=((1,), (0,))):
    return lax.dot_general(a, b, (dims, ((), ())), preferred_element_type=jnp.float32)


def mm(a, b, dims=((1,), (0,))):
    return dot(a[0], b[0], dims) + (dot(a[0], b[1], dims) + dot(a[1], b[0], dims))


def product(a, b):
    terms = [a[:, k : k + 1] * b[k : k + 1, :] for k in range(a.shape[1])]
    while len(terms) > 1:
        terms = [x + y for x, y in zip(terms[::2], terms[1::2])]
    return terms[0]


def diagonal_of(size):
    return lax.broadcasted_iota(jnp.int32, (size, size), 0) == lax.broadcasted_iota(
        jnp.int32, (size, size), 1
    )


def as_column(row, eye):
    return jnp.sum(jnp.where(eye, row, 0.0), axis=1, keepdims=True)


def as_row(column, eye):
    return jnp.sum(jnp.where(eye, column, 0.0), axis=0, keepdims=True)


def solve(gram, innovation, weight, eye, members):
    nobs = gram.shape[0]
    weight_col = as_column(weight, eye)
    trace = jnp.sum(jnp.where(eye, gram * weight, 0.0), axis=(0, 1), keepdims=True)
    inverse = 1.0 / (members - 1.0 + 0.5 * trace)
    a = (members - 1.0) * inverse
    t = gram * (weight * inverse)
    identity = jnp.where(eye, 1.0, 0.0)
    group = lax.broadcasted_iota(jnp.int32, (nobs, 4 * nobs), 1) // nobs
    state = jnp.concatenate([a * identity + t, identity, identity, jnp.zeros_like(t)], axis=1)
    p0, z0 = a, jnp.ones_like(a)
    for repeat in range(NSI):
        g0 = 1.5 - 0.5 * p0
        g = 1.5 * identity - 0.5 * state[:, :nobs]
        h = state[:, nobs : 2 * nobs]
        spread_h = jnp.concatenate([h, h, h, h], axis=1)
        along = jnp.where(group == 1, -0.5 * p0, jnp.where(group == 3, -0.5 * z0, 0.0))
        state = product(g, state) + along * spread_h
        z0 = z0 * g0
        if repeat < NSI - 1:
            again = product(g, state) + jnp.where(group == 1, -0.5 * p0 * g0, 0.0) * spread_h
            state = jnp.where(group < 2, again, state)
            p0 = p0 * g0 * g0
    z = state[:, 2 * nobs : 3 * nobs]
    root = jnp.sqrt(a)
    shift = weight_col * product(z, product(z, innovation)) * inverse
    return root * z0, (root * inverse) * weight_col * state[:, 3 * nobs :], shift


def kernel(
    x_hbm, values_hbm, variance_hbm, cell_hbm, loop_hbm, count_hbm, o_ref,
    x_ref, values_ref, variance_ref, cell_ref, loop_ref, count_ref, wide, mid, mid2, packed, gathered, fresh, centred, back,
    halo_send, halo_recv, send_a, recv_a, send_b, recv_b, load_x, load_small,
):
    n_mem, n_lat = lax.axis_size("mem"), lax.axis_size("lat")
    me, band = lax.axis_index("mem"), lax.axis_index("lat")
    members, fields, _, _ = x_hbm.shape
    rows = 4
    chunks = members // CHUNK
    spans = packed.shape[2]
    held = fields // spans

    loads = [
        pltpu.make_async_copy(
            x_hbm.at[pl.ds(c * CHUNK, CHUNK)], x_ref.at[pl.ds(c * CHUNK, CHUNK)], load_x.at[c]
        )
        for c in range(chunks)
    ]
    small = [
        pltpu.make_async_copy(source, target, load_small.at[k])
        for k, (source, target) in enumerate(
            (
                (values_hbm, values_ref), (variance_hbm, variance_ref), (cell_hbm, cell_ref),
                (loop_hbm, loop_ref), (count_hbm, count_ref),
            )
        )
    ]
    for load in loads + small:
        load.start()

    ring = n_mem // 4
    my_y = me // 4
    my_x = (me - 4 * my_y) // 2
    my_core = me - 4 * my_y - 2 * my_x
    ys = [my_y] + [jnp.where(my_y + k >= ring, my_y + k - ring, my_y + k) for k in range(1, ring)]
    xs = (my_x, 1 - my_x)
    cores = (my_core, 1 - my_core)
    order = [ring // 2]
    for k in range(1, ring // 2):
        order += [ring // 2 - k, ring // 2 + k]
    peers = [
        (ys[k], 2 * xs[x] + cores[core])
        for k in order + [0]
        for x, core in ((1, 1), (1, 0), (0, 1), (0, 0))
        if k or x or core
    ]

    barrier = pltpu.get_barrier_semaphore()

    @pl.when(band < n_lat - 1)
    def _():
        pl.semaphore_signal(barrier, inc=1, device_id={"lat": band + 1}, device_id_type=MESH)

    @pl.when(band > 0)
    def _():
        pl.semaphore_signal(barrier, inc=1, device_id={"lat": band - 1}, device_id_type=MESH)

    for y, q in peers:
        pl.semaphore_signal(barrier, inc=1, device_id={"mem": 4 * y + q}, device_id_type=MESH)

    def spread_rows(c):
        loads[c].wait()
        for m in range(c * CHUNK, (c + 1) * CHUNK):
            for f in range(fields):
                for r in range(rows):
                    wide[m, HALO + r, f] = x_ref[m, f, pl.ds(r, 8, stride=rows), :]

    spread_rows(0)
    beside = (band + n_lat - 1) // n_lat + (2 * n_lat - 2 - band) // n_lat
    pl.semaphore_wait(barrier, n_mem - 1 + beside)

    def upward(c):
        part = pl.ds(c * CHUNK, CHUNK)
        return pltpu.make_async_remote_copy(
            src_ref=wide.at[part, pl.ds(rows, HALO)], dst_ref=wide.at[part, pl.ds(0, HALO)],
            send_sem=halo_send.at[0, c], recv_sem=halo_recv.at[0, c],
            device_id={"lat": band + 1}, device_id_type=MESH,
        )

    def downward(c):
        part = pl.ds(c * CHUNK, CHUNK)
        return pltpu.make_async_remote_copy(
            src_ref=wide.at[part, pl.ds(HALO, HALO)], dst_ref=wide.at[part, pl.ds(HALO + rows, HALO)],
            send_sem=halo_send.at[1, c], recv_sem=halo_recv.at[1, c],
            device_id={"lat": band - 1}, device_id_type=MESH,
        )

    for c in range(chunks):
        if c:
            spread_rows(c)

        @pl.when(band < n_lat - 1)
        def _():
            upward(c).start()

        @pl.when(band > 0)
        def _():
            downward(c).start()

    lane = lax.broadcasted_iota(jnp.int32, (8, 128), 1)
    last_lane, first_lane = lane == 127, lane == 0
    quarter = lane // 32
    has_south, has_north = band > 0, band < n_lat - 1

    def east(c):
        turned = pltpu.roll(c, 127, 1)
        return jnp.where(last_lane, pltpu.roll(turned, 7, 0), turned)

    def west(c):
        turned = pltpu.roll(c, 1, 1)
        return jnp.where(first_lane, pltpu.roll(turned, 1, 0), turned)

    def stage(source, base, count, weight_base, weight_mid):
        scale = weight_mid * DT
        for i in range(count):
            u = 0.5 * scale * source(i + 1, 0)
            v = 0.5 * scale * source(i + 1, 1)
            drag = scale * VISC
            east_w, west_w, north_w, south_w = drag - u, drag + u, drag - v, drag + v
            for f in range(fields):
                c = source(i + 1, f)
                total = (weight_mid - 4.0 * drag) * c
                total += north_w * source(i + 2, f) + south_w * source(i, f)
                total += east_w * east(c) + west_w * west(c)
                if weight_base:
                    total += weight_base * base(i, f)
                yield i, f, total

    def inside(value, i, extra):
        if i < extra:
            return jnp.where(has_south, value, 0.0)
        if i >= extra + rows:
            return jnp.where(has_north, value, 0.0)
        return value

    def advance_member(c, ml):
        m = c * CHUNK + ml

        def from_wide(i, f):
            return inside(wide[m, i, f], i, HALO)

        for i, f, value in stage(from_wide, None, rows + 4, 0.0, 1.0):
            mid[i, f] = inside(value, i, 2)
        for i, f, value in stage(lambda i, f: mid[i, f], lambda i, f: from_wide(i + 2, f), rows + 2, 0.75, 0.25):
            mid2[i, f] = inside(value, i, 1)
        result = {}
        for i, f, value in stage(lambda i, f: mid2[i, f], lambda i, f: wide[m, i + 3, f], rows, 1.0 / 3.0, 2.0 / 3.0):
            result[i, f] = value
        for f in range(fields):
            pieces = [result[r, f] for r in range(rows)]
            for q in range(rows):
                packed[c, q, f // held, pl.ds(ml * held + f % held, 8, stride=8), :] = choose(pieces, q, quarter)

    mine, others = pl.ds(pl.multiple_of(me * 8, 8), 8), pl.ds(0, (n_mem - 1) * 8)
    my_q, my_rows = me - 4 * my_y, pl.ds(pl.multiple_of(my_y * 8, 8), 8)

    def chunk_step(c, _):
        @pl.when(has_south)
        def _():
            upward(c).wait_recv()

        @pl.when(has_north)
        def _():
            downward(c).wait_recv()

        for ml in range(CHUNK):
            advance_member(c, ml)

        for y, q in peers:
            pltpu.make_async_remote_copy(
                src_ref=packed.at[c, q, :, pl.ds(pl.multiple_of(y * 8, 8), 8)], dst_ref=gathered.at[c, :, mine],
                send_sem=send_a.at[c], recv_sem=recv_a.at[c],
                device_id={"mem": 4 * y + q}, device_id_type=MESH,
            ).start()

        gathered[c, :, mine] = packed[c, my_q, :, my_rows]
        return 0

    lax.fori_loop(0, chunks, chunk_step, 0)

    for load in small:
        load.wait()
    nobs = values_ref.shape[1]
    eye = diagonal_of(nobs)
    cells = fields * 128
    cell_col = as_column(cell_ref[...].astype(jnp.float32), eye).astype(jnp.int32)
    is_cell = lax.broadcasted_iota(jnp.int32, (nobs, cells), 1) == cell_col
    onehot = jnp.where(is_cell, 1.0, 0.0)
    pick = onehot.astype(jnp.bfloat16)
    slots = lax.broadcasted_iota(jnp.int32, (1, nobs), 1)
    decay = jnp.exp(-0.35 * loop_ref[...].astype(jnp.float32)) / variance_ref[...]
    weight = jnp.where(slots < count_ref[...], decay, 0.0)

    total = n_mem * members
    size = n_mem * CHUNK
    seen_parts = []
    for c in range(chunks):
        pltpu.make_async_copy(gathered.at[c, :, others], gathered.at[c, :, others], recv_a.at[c]).wait()
        block = jnp.concatenate(
            [gathered[c, f // held, pl.ds(f % held, size, stride=held), :] for f in range(fields)], axis=1
        )
        if c == 0:
            origin = jnp.sum(block, axis=0, keepdims=True) * (1.0 / size)
        moved = block - origin
        centred[c] = moved
        parts = split(moved)
        seen = dot(parts[0], pick, ((1,), (1,))) + dot(parts[1], pick, ((1,), (1,)))
        seen_t = dot(pick, parts[0], ((1,), (1,))) + dot(pick, parts[1], ((1,), (1,)))
        turned = split(seen_t)
        seen_parts.append(split(seen))
        cross_c = mm(turned, parts)
        gram_c = mm(turned, turned, ((1,), (1,)))
        sum_c = jnp.sum(moved, axis=0, keepdims=True)
        if c == 0:
            cross, gram, summed = cross_c, gram_c, sum_c
        else:
            cross, gram, summed = cross + cross_c, gram + gram_c, summed + sum_c

    offset = summed * (1.0 / total)
    offset_seen = jnp.sum(onehot * offset, axis=1, keepdims=True)
    origin_seen = jnp.sum(onehot * origin, axis=1, keepdims=True)
    cross = cross - (float(total) * offset_seen) * offset
    gram = gram - (float(total) * offset_seen) * as_row(offset_seen, eye)
    innovation = as_column(values_ref[...], eye) - (origin_seen + offset_seen)
    kept, on_cross, shift = solve(gram, innovation, weight, eye, float(total))
    rows_seen = product(on_cross, cross)
    common = (
        origin + (1.0 - kept) * offset
        + jnp.sum(shift * cross - offset_seen * rows_seen, axis=0, keepdims=True)
    )
    rows_parts = split(rows_seen)
    for c in range(chunks):
        updated = kept * centred[c] + (mm(seen_parts[c], rows_parts) + common)
        for f in range(fields):
            fresh[c, f // held, pl.ds(f % held, size, stride=held), :] = updated[:, f * 128 : (f + 1) * 128]

    for y, q in peers:
        place = pl.ds(pl.multiple_of((4 * y + q) * 8, 8), 8)
        pltpu.make_async_remote_copy(
            src_ref=fresh.at[:, :, place], dst_ref=back.at[:, my_q, :, my_rows],
            send_sem=send_b.at[0], recv_sem=recv_b.at[0],
            device_id={"mem": 4 * y + q}, device_id_type=MESH,
        ).start()
    back[:, my_q, :, my_rows] = fresh[:, :, mine]

    for c in range(chunks):
        pltpu.make_async_copy(gathered.at[c, :, others], gathered.at[c, :, others], send_a.at[c]).wait()

    @pl.when(has_north)
    def _():
        for c in range(chunks):
            upward(c).wait_send()

    @pl.when(has_south)
    def _():
        for c in range(chunks):
            downward(c).wait_send()

    pltpu.make_async_copy(fresh.at[:, :, others], fresh.at[:, :, others], recv_b.at[0]).wait()
    for c in range(chunks):
        for ml in range(CHUNK):
            for f in range(fields):
                pieces = [back[c, q, f // held, pl.ds(ml * held + f % held, 8, stride=8), :] for q in range(rows)]
                for r in range(rows):
                    o_ref[c * CHUNK + ml, f, pl.ds(r, 8, stride=rows), :] = choose(pieces, r, quarter)

    pltpu.make_async_copy(fresh.at[:, :, others], fresh.at[:, :, others], send_b.at[0]).wait()


def per_device(ensemble, obs_value, obs_var, obs_cell, obs_loop, obs_count):
    members, fields, rows, width = ensemble.shape
    n_mem = lax.axis_size("mem")
    f32 = jnp.float32
    nobs = obs_value.shape[2]
    blocks = width // 128
    chunks = members // CHUNK
    spans = fields * CHUNK // 8
    view = (
        ensemble.reshape(members, fields, rows, blocks, 128)
        .transpose(0, 1, 3, 2, 4)
        .reshape(members, fields, blocks * rows, 128)
    )
    out = pl.pallas_call(
        kernel,
        out_shape=pltpu.VMEM(view.shape, f32),
        in_specs=[pl.BlockSpec(memory_space=pl.ANY)] * 6,
        out_specs=pl.BlockSpec(memory_space=pltpu.VMEM),
        scratch_shapes=[
            pltpu.VMEM(view.shape, f32),
            pltpu.VMEM((1, nobs), f32),
            pltpu.VMEM((1, nobs), f32),
            pltpu.VMEM((1, nobs), jnp.int32),
            pltpu.VMEM((1, nobs), jnp.int32),
            pltpu.VMEM((1, 1), jnp.int32),
            pltpu.VMEM((members, rows + 2 * HALO, fields, 8, 128), f32),
            pltpu.VMEM((rows + 4, fields, 8, 128), f32),
            pltpu.VMEM((rows + 2, fields, 8, 128), f32),
            pltpu.VMEM((chunks, rows, spans, 64, 128), f32),
            pltpu.VMEM((chunks, spans, n_mem * 8, 128), f32),
            pltpu.VMEM((chunks, spans, n_mem * 8, 128), f32),
            pltpu.VMEM((chunks, n_mem * CHUNK, fields * 128), f32),
            pltpu.VMEM((chunks, rows, spans, 64, 128), f32),
            pltpu.SemaphoreType.DMA((2, chunks)),
            pltpu.SemaphoreType.DMA((2, chunks)),
            pltpu.SemaphoreType.DMA((chunks,)),
            pltpu.SemaphoreType.DMA((chunks,)),
            pltpu.SemaphoreType.DMA((chunks,)),
            pltpu.SemaphoreType.DMA((chunks,)),
            pltpu.SemaphoreType.DMA((chunks,)),
            pltpu.SemaphoreType.DMA((5,)),
        ],
        compiler_params=pltpu.CompilerParams(collective_id=0, has_side_effects=True),
    )(
        view, obs_value[0], obs_var[0], obs_cell[0], obs_loop[0], obs_count,
    )
    return (
        out.reshape(members, fields, blocks, rows, 128)
        .transpose(0, 1, 3, 2, 4)
        .reshape(ensemble.shape)
    )


def solution(mesh):
    placed = (
        P("mem", None, "lat", None),
        P(None, ("mem", "lat"), None),
        P(None, ("mem", "lat"), None),
        P(None, ("mem", "lat"), None),
        P(None, ("mem", "lat"), None),
        P(None, ("mem", "lat")),
    )
    return jax.shard_map(
        per_device,
        mesh=mesh,
        in_specs=placed,
        out_specs=P("mem", None, "lat", None),
        check_vma=False,
    )
```

```python
import jax
import jax.numpy as jnp
from jax import lax
from jax.experimental import pallas as pl
from jax.experimental.pallas import tpu as pltpu
from jax.sharding import PartitionSpec as P

MESH = pl.DeviceIdType.MESH
NSI = 5
DT = 0.15
VISC = 0.1
CHUNK = 1
HALO = 3


def choose(pieces, offset, quarter):
    out = None
    for r, piece in enumerate(pieces):
        turned = pltpu.roll(piece, ((r - offset) * 32) % 128, 1) if r != offset else piece
        out = turned if out is None else jnp.where(quarter == r, turned, out)
    return out


def split(x):
    high = x.astype(jnp.bfloat16)
    return high, (x - high.astype(jnp.float32)).astype(jnp.bfloat16)


def dot(a, b, dims=((1,), (0,))):
    return lax.dot_general(a, b, (dims, ((), ())), preferred_element_type=jnp.float32)


def mm(a, b, dims=((1,), (0,))):
    return dot(a[0], b[0], dims) + (dot(a[0], b[1], dims) + dot(a[1], b[0], dims))


def product(a, b):
    terms = [a[:, k : k + 1] * b[k : k + 1, :] for k in range(a.shape[1])]
    while len(terms) > 1:
        terms = [x + y for x, y in zip(terms[::2], terms[1::2])]
    return terms[0]


def diagonal_of(size):
    return lax.broadcasted_iota(jnp.int32, (size, size), 0) == lax.broadcasted_iota(
        jnp.int32, (size, size), 1
    )


def as_column(row, eye):
    return jnp.sum(jnp.where(eye, row, 0.0), axis=1, keepdims=True)


def as_row(column, eye):
    return jnp.sum(jnp.where(eye, column, 0.0), axis=0, keepdims=True)


def solve(gram, innovation, weight, eye, members):
    nobs = gram.shape[0]
    weight_col = as_column(weight, eye)
    trace = jnp.sum(jnp.where(eye, gram * weight, 0.0), axis=(0, 1), keepdims=True)
    inverse = 1.0 / (members - 1.0 + 0.5 * trace)
    a = (members - 1.0) * inverse
    t = gram * (weight * inverse)
    identity = jnp.where(eye, 1.0, 0.0)
    group = lax.broadcasted_iota(jnp.int32, (nobs, 4 * nobs), 1) // nobs
    state = jnp.concatenate([a * identity + t, identity, identity, jnp.zeros_like(t)], axis=1)
    p0, z0 = a, jnp.ones_like(a)
    for repeat in range(NSI):
        g0 = 1.5 - 0.5 * p0
        g = 1.5 * identity - 0.5 * state[:, :nobs]
        h = state[:, nobs : 2 * nobs]
        spread_h = jnp.concatenate([h, h, h, h], axis=1)
        along = jnp.where(group == 1, -0.5 * p0, jnp.where(group == 3, -0.5 * z0, 0.0))
        state = product(g, state) + along * spread_h
        z0 = z0 * g0
        if repeat < NSI - 1:
            again = product(g, state) + jnp.where(group == 1, -0.5 * p0 * g0, 0.0) * spread_h
            state = jnp.where(group < 2, again, state)
            p0 = p0 * g0 * g0
    z = state[:, 2 * nobs : 3 * nobs]
    root = jnp.sqrt(a)
    shift = weight_col * product(z, product(z, innovation)) * inverse
    return root * z0, (root * inverse) * weight_col * state[:, 3 * nobs :], shift


def kernel(
    x_hbm, values_hbm, variance_hbm, cell_hbm, loop_hbm, count_hbm, o_ref,
    x_ref, values_ref, variance_ref, cell_ref, loop_ref, count_ref, wide, mid, mid2, packed, gathered, fresh, centred, back,
    halo_send, halo_recv, send_a, recv_a, send_b, recv_b, load_x, load_small,
):
    n_mem, n_lat = lax.axis_size("mem"), lax.axis_size("lat")
    me, band = lax.axis_index("mem"), lax.axis_index("lat")
    members, fields, _, _ = x_hbm.shape
    rows = 4
    chunks = members // CHUNK
    spans = packed.shape[2]
    held = fields // spans
    tile = CHUNK * held

    loads = [
        pltpu.make_async_copy(
            x_hbm.at[pl.ds(c * CHUNK, CHUNK)], x_ref.at[pl.ds(c * CHUNK, CHUNK)], load_x.at[c]
        )
        for c in range(chunks)
    ]
    small = [
        pltpu.make_async_copy(source, target, load_small.at[k])
        for k, (source, target) in enumerate(
            (
                (values_hbm, values_ref), (variance_hbm, variance_ref), (cell_hbm, cell_ref),
                (loop_hbm, loop_ref), (count_hbm, count_ref),
            )
        )
    ]
    for load in loads + small:
        load.start()

    ring = n_mem // 4
    my_y = me // 4
    my_x = (me - 4 * my_y) // 2
    my_core = me - 4 * my_y - 2 * my_x
    ys = [my_y] + [jnp.where(my_y + k >= ring, my_y + k - ring, my_y + k) for k in range(1, ring)]
    xs = (my_x, 1 - my_x)
    cores = (my_core, 1 - my_core)
    order = [ring // 2]
    for k in range(1, ring // 2):
        order += [ring // 2 - k, ring // 2 + k]
    peers = [
        (ys[k], 2 * xs[x] + cores[core])
        for k in order + [0]
        for x, core in ((1, 1), (1, 0), (0, 1), (0, 0))
        if k or x or core
    ]

    barrier = pltpu.get_barrier_semaphore()

    @pl.when(band < n_lat - 1)
    def _():
        pl.semaphore_signal(barrier, inc=1, device_id={"lat": band + 1}, device_id_type=MESH)

    @pl.when(band > 0)
    def _():
        pl.semaphore_signal(barrier, inc=1, device_id={"lat": band - 1}, device_id_type=MESH)

    for y, q in peers:
        pl.semaphore_signal(barrier, inc=1, device_id={"mem": 4 * y + q}, device_id_type=MESH)

    def spread_rows(c):
        loads[c].wait()
        for m in range(c * CHUNK, (c + 1) * CHUNK):
            for f in range(fields):
                for r in range(rows):
                    wide[m, HALO + r, f] = x_ref[m, f, pl.ds(r, 8, stride=rows), :]

    spread_rows(0)
    beside = (band + n_lat - 1) // n_lat + (2 * n_lat - 2 - band) // n_lat
    pl.semaphore_wait(barrier, n_mem - 1 + beside)

    def upward(c):
        part = pl.ds(c * CHUNK, CHUNK)
        return pltpu.make_async_remote_copy(
            src_ref=wide.at[part, pl.ds(rows, HALO)], dst_ref=wide.at[part, pl.ds(0, HALO)],
            send_sem=halo_send.at[0, c], recv_sem=halo_recv.at[0, c],
            device_id={"lat": band + 1}, device_id_type=MESH,
        )

    def downward(c):
        part = pl.ds(c * CHUNK, CHUNK)
        return pltpu.make_async_remote_copy(
            src_ref=wide.at[part, pl.ds(HALO, HALO)], dst_ref=wide.at[part, pl.ds(HALO + rows, HALO)],
            send_sem=halo_send.at[1, c], recv_sem=halo_recv.at[1, c],
            device_id={"lat": band - 1}, device_id_type=MESH,
        )

    for c in range(chunks):
        if c:
            spread_rows(c)

        @pl.when(band < n_lat - 1)
        def _():
            upward(c).start()

        @pl.when(band > 0)
        def _():
            downward(c).start()

    lane = lax.broadcasted_iota(jnp.int32, (8, 128), 1)
    last_lane, first_lane = lane == 127, lane == 0
    quarter = lane // 32
    has_south, has_north = band > 0, band < n_lat - 1

    def east(c):
        turned = pltpu.roll(c, 127, 1)
        return jnp.where(last_lane, pltpu.roll(turned, 7, 0), turned)

    def west(c):
        turned = pltpu.roll(c, 1, 1)
        return jnp.where(first_lane, pltpu.roll(turned, 1, 0), turned)

    def stage(source, base, count, weight_base, weight_mid):
        scale = weight_mid * DT
        for i in range(count):
            u = 0.5 * scale * source(i + 1, 0)
            v = 0.5 * scale * source(i + 1, 1)
            drag = scale * VISC
            east_w, west_w, north_w, south_w = drag - u, drag + u, drag - v, drag + v
            for f in range(fields):
                c = source(i + 1, f)
                total = (weight_mid - 4.0 * drag) * c
                total += north_w * source(i + 2, f) + south_w * source(i, f)
                total += east_w * east(c) + west_w * west(c)
                if weight_base:
                    total += weight_base * base(i, f)
                yield i, f, total

    def inside(value, i, extra):
        if i < extra:
            return jnp.where(has_south, value, 0.0)
        if i >= extra + rows:
            return jnp.where(has_north, value, 0.0)
        return value

    def advance_member(c, ml):
        m = c * CHUNK + ml

        def from_wide(i, f):
            return inside(wide[m, i, f], i, HALO)

        for i, f, value in stage(from_wide, None, rows + 4, 0.0, 1.0):
            mid[i, f] = inside(value, i, 2)
        for i, f, value in stage(lambda i, f: mid[i, f], lambda i, f: from_wide(i + 2, f), rows + 2, 0.75, 0.25):
            mid2[i, f] = inside(value, i, 1)
        result = {}
        for i, f, value in stage(lambda i, f: mid2[i, f], lambda i, f: wide[m, i + 3, f], rows, 1.0 / 3.0, 2.0 / 3.0):
            result[i, f] = value
        for f in range(fields):
            pieces = [result[r, f] for r in range(rows)]
            for q in range(rows):
                packed[c, q, f // held, pl.ds(ml * held + f % held, 8, stride=tile), :] = choose(pieces, q, quarter)

    mine, others = pl.ds(pl.multiple_of(me * tile, tile), tile), pl.ds(0, (n_mem - 1) * tile)
    my_q, my_rows = me - 4 * my_y, pl.ds(pl.multiple_of(my_y * tile, tile), tile)

    def chunk_step(c, _):
        @pl.when(has_south)
        def _():
            upward(c).wait_recv()

        @pl.when(has_north)
        def _():
            downward(c).wait_recv()

        for ml in range(CHUNK):
            advance_member(c, ml)

        for y, q in peers:
            pltpu.make_async_remote_copy(
                src_ref=packed.at[c, q, :, pl.ds(pl.multiple_of(y * tile, tile), tile)], dst_ref=gathered.at[c, :, mine],
                send_sem=send_a.at[c], recv_sem=recv_a.at[c],
                device_id={"mem": 4 * y + q}, device_id_type=MESH,
            ).start()

        gathered[c, :, mine] = packed[c, my_q, :, my_rows]
        return 0

    lax.fori_loop(0, chunks, chunk_step, 0)

    for load in small:
        load.wait()
    nobs = values_ref.shape[1]
    eye = diagonal_of(nobs)
    cells = fields * 128
    cell_col = as_column(cell_ref[...].astype(jnp.float32), eye).astype(jnp.int32)
    is_cell = lax.broadcasted_iota(jnp.int32, (nobs, cells), 1) == cell_col
    onehot = jnp.where(is_cell, 1.0, 0.0)
    pick = onehot.astype(jnp.bfloat16)
    slots = lax.broadcasted_iota(jnp.int32, (1, nobs), 1)
    decay = jnp.exp(-0.35 * loop_ref[...].astype(jnp.float32)) / variance_ref[...]
    weight = jnp.where(slots < count_ref[...], decay, 0.0)

    total = n_mem * members
    size = n_mem * CHUNK
    seen_parts = []
    for c in range(chunks):
        pltpu.make_async_copy(gathered.at[c, :, others], gathered.at[c, :, others], recv_a.at[c]).wait()
        block = jnp.concatenate(
            [gathered[c, f // held, pl.ds(f % held, size, stride=held), :] for f in range(fields)], axis=1
        )
        if c == 0:
            origin = jnp.sum(block, axis=0, keepdims=True) * (1.0 / size)
        moved = block - origin
        centred[c] = moved
        parts = split(moved)
        seen = dot(parts[0], pick, ((1,), (1,))) + dot(parts[1], pick, ((1,), (1,)))
        seen_t = dot(pick, parts[0], ((1,), (1,))) + dot(pick, parts[1], ((1,), (1,)))
        turned = split(seen_t)
        seen_parts.append(split(seen))
        cross_c = mm(turned, parts)
        gram_c = mm(turned, turned, ((1,), (1,)))
        sum_c = jnp.sum(moved, axis=0, keepdims=True)
        if c == 0:
            cross, gram, summed = cross_c, gram_c, sum_c
        else:
            cross, gram, summed = cross + cross_c, gram + gram_c, summed + sum_c

    offset = summed * (1.0 / total)
    offset_seen = jnp.sum(onehot * offset, axis=1, keepdims=True)
    origin_seen = jnp.sum(onehot * origin, axis=1, keepdims=True)
    cross = cross - (float(total) * offset_seen) * offset
    gram = gram - (float(total) * offset_seen) * as_row(offset_seen, eye)
    innovation = as_column(values_ref[...], eye) - (origin_seen + offset_seen)
    kept, on_cross, shift = solve(gram, innovation, weight, eye, float(total))
    rows_seen = product(on_cross, cross)
    common = (
        origin + (1.0 - kept) * offset
        + jnp.sum(shift * cross - offset_seen * rows_seen, axis=0, keepdims=True)
    )
    rows_parts = split(rows_seen)
    for c in range(chunks):
        updated = kept * centred[c] + (mm(seen_parts[c], rows_parts) + common)
        for f in range(fields):
            fresh[c, f // held, pl.ds(f % held, size, stride=held), :] = updated[:, f * 128 : (f + 1) * 128]

    for y, q in peers:
        place = pl.ds(pl.multiple_of((4 * y + q) * tile, tile), tile)
        pltpu.make_async_remote_copy(
            src_ref=fresh.at[:, :, place], dst_ref=back.at[:, my_q, :, my_rows],
            send_sem=send_b.at[0], recv_sem=recv_b.at[0],
            device_id={"mem": 4 * y + q}, device_id_type=MESH,
        ).start()
    back[:, my_q, :, my_rows] = fresh[:, :, mine]

    for c in range(chunks):
        pltpu.make_async_copy(gathered.at[c, :, others], gathered.at[c, :, others], send_a.at[c]).wait()

    @pl.when(has_north)
    def _():
        for c in range(chunks):
            upward(c).wait_send()

    @pl.when(has_south)
    def _():
        for c in range(chunks):
            downward(c).wait_send()

    pltpu.make_async_copy(fresh.at[:, :, others], fresh.at[:, :, others], recv_b.at[0]).wait()
    for c in range(chunks):
        for ml in range(CHUNK):
            for f in range(fields):
                pieces = [back[c, q, f // held, pl.ds(ml * held + f % held, 8, stride=tile), :] for q in range(rows)]
                for r in range(rows):
                    o_ref[c * CHUNK + ml, f, pl.ds(r, 8, stride=rows), :] = choose(pieces, r, quarter)

    pltpu.make_async_copy(fresh.at[:, :, others], fresh.at[:, :, others], send_b.at[0]).wait()


def per_device(ensemble, obs_value, obs_var, obs_cell, obs_loop, obs_count):
    members, fields, rows, width = ensemble.shape
    n_mem = lax.axis_size("mem")
    f32 = jnp.float32
    nobs = obs_value.shape[2]
    blocks = width // 128
    chunks = members // CHUNK
    spans = max(1, fields * CHUNK // 8)
    tile = CHUNK * fields // spans
    view = (
        ensemble.reshape(members, fields, rows, blocks, 128)
        .transpose(0, 1, 3, 2, 4)
        .reshape(members, fields, blocks * rows, 128)
    )
    out = pl.pallas_call(
        kernel,
        out_shape=pltpu.VMEM(view.shape, f32),
        in_specs=[pl.BlockSpec(memory_space=pl.ANY)] * 6,
        out_specs=pl.BlockSpec(memory_space=pltpu.VMEM),
        scratch_shapes=[
            pltpu.VMEM(view.shape, f32),
            pltpu.VMEM((1, nobs), f32),
            pltpu.VMEM((1, nobs), f32),
            pltpu.VMEM((1, nobs), jnp.int32),
            pltpu.VMEM((1, nobs), jnp.int32),
            pltpu.VMEM((1, 1), jnp.int32),
            pltpu.VMEM((members, rows + 2 * HALO, fields, 8, 128), f32),
            pltpu.VMEM((rows + 4, fields, 8, 128), f32),
            pltpu.VMEM((rows + 2, fields, 8, 128), f32),
            pltpu.VMEM((chunks, rows, spans, 8 * tile, 128), f32),
            pltpu.VMEM((chunks, spans, n_mem * tile, 128), f32),
            pltpu.VMEM((chunks, spans, n_mem * tile, 128), f32),
            pltpu.VMEM((chunks, n_mem * CHUNK, fields * 128), f32),
            pltpu.VMEM((chunks, rows, spans, 8 * tile, 128), f32),
            pltpu.SemaphoreType.DMA((2, chunks)),
            pltpu.SemaphoreType.DMA((2, chunks)),
            pltpu.SemaphoreType.DMA((chunks,)),
            pltpu.SemaphoreType.DMA((chunks,)),
            pltpu.SemaphoreType.DMA((chunks,)),
            pltpu.SemaphoreType.DMA((chunks,)),
            pltpu.SemaphoreType.DMA((chunks,)),
            pltpu.SemaphoreType.DMA((5,)),
        ],
        compiler_params=pltpu.CompilerParams(collective_id=0, has_side_effects=True),
    )(
        view, obs_value[0], obs_var[0], obs_cell[0], obs_loop[0], obs_count,
    )
    return (
        out.reshape(members, fields, blocks, rows, 128)
        .transpose(0, 1, 3, 2, 4)
        .reshape(ensemble.shape)
    )


def solution(mesh):
    placed = (
        P("mem", None, "lat", None),
        P(None, ("mem", "lat"), None),
        P(None, ("mem", "lat"), None),
        P(None, ("mem", "lat"), None),
        P(None, ("mem", "lat"), None),
        P(None, ("mem", "lat")),
    )
    return jax.shard_map(
        per_device,
        mesh=mesh,
        in_specs=placed,
        out_specs=P("mem", None, "lat", None),
        check_vma=False,
    )
```
